32 devices in a mesh: clip: 4 (over z), sp: 4 (over x, core), tp: 2 (over y).
Axes of the slice: x: 2, y: 2, z: 4, core: 2. Of those that a mesh axis runs over, the one named last changes fastest.
Arguments:
- latents: bfloat16 [4, 4, 1024, 512], P('clip', 'sp', None, 'tp'), may hold values from -6 to 6
- saved_input: bfloat16 [4, 4, 1024, 512], P('clip', None, 'sp', 'tp'), may hold values from -6 to 6
- out_grad: bfloat16 [4, 4, 1024, 512], P('clip', None, 'sp', 'tp'), may hold values from -6 to 6
- temporal_weight: bfloat16 [3, 512, 512], P(None, 'tp'), may hold values from -0.15625 to 0.15625
- spatial_weight: bfloat16 [9, 512, 512], P(None, 'tp'), may hold values from -0.09375 to 0.09375
Outputs:
- input_grad: bfloat16 [4, 4, 1024, 512], P('clip', 'sp', None, 'tp')
- temporal_grad: float32 [3, 512, 512], P(None, 'tp', 'sp')
- spatial_grad: float32 [9, 512, 512], P(None, 'tp', 'sp')
The draws below stay inside these ranges and needn't reach their ends.
All inputs are finite; a program needn't handle non-finite values.
Results may differ from the reference program's by a relative error of at most 0.005.
Values may be sent and summed in bfloat16 or wider, within the bound.
A program may use at most 64 MiB of HBM per device.

```python
import jax
import jax.numpy as jnp
from jax import lax

C = 512
HS = 32
WS = 32
FRAMES = 4
CLIPS = 4
HW = 1024


def with_spikes(values, rng, source, target, blocks, factor):
    owner, partner = [(jnp.arange(values.shape[axis_at]) // (values.shape[axis_at] // blocks)).reshape([-1 if axis == axis_at else 1 for axis in range(values.ndim)]) for axis_at in (source, target)]
    chosen = jax.random.permutation(rng, blocks)[partner]
    strong = (owner == chosen) | (owner == (partner + blocks // 2) % blocks)
    return jnp.where(strong, factor * values, values)


def steps_of(stream_key, dims, split, low, top_value):
    factor_of, own = 1.0, jax.random.fold_in(stream_key, 6)
    for axis_at, parts in split:
        heights = jnp.exp(jax.random.uniform(jax.random.fold_in(own, axis_at), (parts,), jnp.float32, low / len(split), top_value / len(split)))
        factor_of = factor_of * jnp.repeat(heights, dims[axis_at] // parts).reshape([-1 if axis == axis_at else 1 for axis in range(len(dims))])
    return factor_of


def noise(key, extent, scale, limit, cuts=(), kind=jnp.bfloat16):
    factor_of = steps_of(key, extent, cuts, -0.22, 0.18) if cuts else 1.0
    values = jax.random.normal(key, extent, jnp.float32) * scale * factor_of
    return jnp.minimum(jnp.maximum(values, -limit), limit).astype(kind)


def heavy_noise(stream_key, shape, scale, limit, shards, heavy, dtype=jnp.bfloat16):
    array = scale * jax.random.normal(stream_key, shape, jnp.float32)
    if shards:
        array = array * steps_of(stream_key, shape, shards, -0.22, 0.18)
    return jnp.clip(with_spikes(array, jax.random.fold_in(stream_key, 3), *heavy), -limit, limit).astype(dtype)


def setup_inputs(seed: int = 0) -> dict:
    splits = jax.random.split(jax.random.key(seed), 6)
    return {
        "latents": noise(splits[0], (CLIPS, FRAMES, HW, C), 1.0, 6.0, ((0, 4), (1, 4), (3, 2))),
        "saved_input": noise(splits[1], (CLIPS, FRAMES, HW, C), 1.0, 6.0, ((0, 4), (2, 4), (3, 2))),
        "out_grad": heavy_noise(splits[2], (CLIPS, FRAMES, HW, C), 1.0, 6.0, ((0, 4), (2, 4), (3, 2)), (2, 3, 4, 2.0)),
        "temporal_weight": noise(splits[3], (3, C, C), (3 * C) ** -0.5, 0.15625, ((1, 2),)),
        "spatial_weight": noise(splits[4], (9, C, C), (9 * C) ** -0.5, 0.09375, ((1, 2),)),
    }


def reference(latents, saved_input, out_grad, temporal_weight, spatial_weight):
    clips, frames, cells, width = latents.shape
    temporal_full = temporal_weight.astype(jnp.float32)
    spatial_full = spatial_weight.astype(jnp.float32)

    def one_clip(index):
        grad_out = out_grad[index].astype(jnp.float32)
        saved = saved_input[index].astype(jnp.float32)
        image = latents[index].astype(jnp.float32)
        grad_pad = jnp.pad(grad_out, ((1, 1), (0, 0), (0, 0)))
        saved_pad = jnp.pad(saved, ((1, 1), (0, 0), (0, 0)))
        hidden_acc = jnp.zeros((frames, cells, width), jnp.float32)
        temporal_parts = []
        for tap_index in range(3):
            shifted = grad_pad[2 - tap_index:2 - tap_index + frames]
            hidden_acc = hidden_acc + jnp.einsum('fpo,io->fpi', shifted, temporal_full[tap_index])
            temporal_parts.append(jnp.einsum('fpi,fpo->io', saved_pad[tap_index:tap_index + frames], grad_out))
        hidden_grad = lax.optimization_barrier(hidden_acc.astype(jnp.bfloat16)).astype(jnp.float32)
        grid = jnp.pad(hidden_grad.reshape(frames, HS, WS, width), ((0, 0), (1, 1), (1, 1), (0, 0)))
        image_pad = jnp.pad(image.reshape(frames, HS, WS, width), ((0, 0), (1, 1), (1, 1), (0, 0)))
        plain = hidden_grad.reshape(frames, HS, WS, width)
        input_acc = jnp.zeros((frames, HS, WS, width), jnp.float32)
        spatial_parts = []
        for row_shift in (-1, 0, 1):
            for col_shift in (-1, 0, 1):
                tap_index = 3 * (row_shift + 1) + (col_shift + 1)
                moved = grid[:, 1 - row_shift:1 - row_shift + HS, 1 - col_shift:1 - col_shift + WS]
                input_acc = input_acc + jnp.einsum('gabo,co->gabc', moved, spatial_full[tap_index])
                window = image_pad[:, 1 + row_shift:1 + row_shift + HS, 1 + col_shift:1 + col_shift + WS]
                spatial_parts.append(jnp.einsum('gabc,gabo->co', window, plain))
        result = input_acc.reshape(frames, cells, width).astype(jnp.bfloat16)
        return (result, jnp.stack(temporal_parts), jnp.stack(spatial_parts))
    input_grad, temporal_terms, spatial_terms = lax.map(one_clip, jnp.arange(clips))
    scale_factor = 1.0 / jnp.sqrt(jnp.float32(clips * frames * cells))
    temporal_grad = lax.optimization_barrier(jnp.sum(temporal_terms, axis=0)) * scale_factor
    spatial_grad = lax.optimization_barrier(jnp.sum(spatial_terms, axis=0)) * scale_factor
    return (input_grad, temporal_grad, spatial_grad)
```

```python
import contextlib
import functools
import math

import jax
import jax.numpy as jnp
from jax import lax
from jax.experimental import pallas as pl
from jax.experimental.pallas import tpu as pltpu
from jax.sharding import PartitionSpec as P

HS = 32
WS = 32
MESH = pl.DeviceIdType.MESH
F32 = jnp.float32
BF16 = jnp.bfloat16


def pad_frames(values):
    return jnp.pad(values, ((0, 0), (1, 1), (0, 0), (0, 0)))


def nt(a, b):
    return lax.dot_general(a, b, (((1,), (1,)), ((), ())), preferred_element_type=F32)


def nn(a, b):
    return lax.dot_general(a, b, (((1,), (0,)), ((), ())), preferred_element_type=F32)


scope = contextlib.nullcontext


def pieces_of(taps, parts, rows):
    return [(tap, part * (rows // n), rows // n) for tap, n in zip(taps, parts) for part in range(n)]


def order(chunks, first, images, rows):
    hop, core_hop, link, core = 1.8, 0.7, 1.39, 0.44
    arrival = 9.5
    now, free = 0.0, {"core": 0.0, "x": 2.0, "z": 0.0, "across": 0.0, "back": 0.0}
    pending, out = {}, []

    def send(name, n, step):
        part = chunks[n][2] / rows
        free[name] = max(free[name], now) + (core if name == "core" else link) * part
        pending[step, n] = free[name] + (core_hop if name == "core" else hop)

    taps = list(dict.fromkeys(tap for tap, _, _ in chunks))
    early, late, filler = taps[:first], taps[first:], list(range(images))
    shifted = False
    started = False
    while pending or early or late or filler:
        ready = sorted((at, key) for key, at in pending.items() if at <= now)
        if ready:
            at, (step, n) = ready[0]
            now += 0.08 * chunks[n][2] / rows
            del pending[step, n]
            out.append((step, n))
            if step < 5:
                send(("core", "x", "z", "across", "back")[step], n, step + 1)
            continue
        if not started and not early and now >= arrival:
            started = True
            out.append(("h", 0))
            continue
        soon = min(pending.values()) if pending else 1e9
        if not started and not early:
            soon = min(soon, arrival)
        if early or (started and late):
            if started and not shifted and len(taps) - first - len(late) >= 3:
                shifted = True
                out.append(("s", 0))
                now += 0.5
                continue
            tap = (early or late).pop(0)
            out.append(("g", tap))
            now += 0.45
            for n, chunk in enumerate(chunks):
                if chunk[0] == tap:
                    send("core", n, 1)
        elif started and filler and (soon > now + 0.3 or not pending):
            out.append(("i", filler.pop(0)))
            now += 0.58
        else:
            now = max(now, soon)
    return out


def kernel(
    dims, lat, sav, og, tw, sw, ig, gf,
    latv, savv, twv, swv, opad, hsend, hwide, hs, savt, latt, acc,
    gsend, g1, g2s, g2r, gz, gzf, gzr,
    lsem, osend, orecv, osem, xsend, xrecv, bsend, brecv, ysend, yrecv,
    s1s, s1r, s2s, s2r, s3s, s3r,
):
    S, T, Z, F, Pl, Cl, Cs, chunks, KT = dims
    U = S // 2
    HW = S * Pl
    C = T * Cl
    me_s, me_t, me_z = lax.axis_index("sp"), lax.axis_index("tp"), lax.axis_index("clip")
    me_u, me_c = me_s // 2, lax.rem(me_s, 2)
    sib = me_u * 2 + 1 - me_c
    far = (1 - me_u) * 2
    mate = (me_z, me_s, 1 - me_t)

    loads = [
        pltpu.make_async_copy(src, dst, lsem.at[n])
        for n, (src, dst) in enumerate(((sav, savv), (tw, twv), (lat, latv), (sw, swv)))
    ]
    for copy in (loads[1], loads[0]):
        copy.start()
    my_cols = pl.ds(pl.multiple_of(me_t * Cl, Cl), Cl)
    mine = [
        pltpu.make_async_copy(og.at[pl.ds(f * Pl, Pl)], opad.at[pl.ds((f + 1) * Pl, Pl), my_cols], osem.at[f])
        for f in range(F)
    ]
    for copy in mine:
        copy.start()
    for copy in (loads[2], loads[3]):
        copy.start()

    with scope("barrier"):
        barrier = pltpu.get_barrier_semaphore()
        peers = [
            mate, (me_z, sib, me_t), (me_z, sib, 1 - me_t), (me_z, far + me_c, me_t), (me_z, far + 1 - me_c, me_t),
        ]
        count = len(peers) + Z - 1
        for peer in peers:
            pl.semaphore_signal(barrier, inc=1, device_id=peer, device_id_type=MESH)
        for dz in range(1, Z):
            pl.semaphore_signal(
                barrier, inc=1, device_id=(lax.rem(me_z + dz, Z), me_s, me_t), device_id_type=MESH
            )
        pl.semaphore_wait(barrier, count)

    def frame(k):
        return jnp.where(me_u == 0, F - 1 - k, k)

    def block(n, base=0):
        return pl.ds(pl.multiple_of(base + n * Pl, 16), Pl)

    ocopies = []
    for k in range(F):
        f = frame(k)
        copy = pltpu.make_async_remote_copy(
            src_ref=og.at[block(f)], dst_ref=opad.at[block(f, Pl), my_cols],
            send_sem=osend.at[k], recv_sem=orecv.at[k], device_id=mate, device_id_type=MESH,
        )
        copy.start()
        ocopies.append(copy)

    opad[pl.ds(0, Pl), :] = jnp.zeros((Pl, C), BF16)
    opad[pl.ds((F + 1) * Pl, Pl), :] = jnp.zeros((Pl, C), BF16)
    hwide[pl.ds(0, 8), :] = jnp.zeros((8, C), F32)
    hwide[pl.ds(8 + HW, 8), :] = jnp.zeros((8, C), F32)
    for b in range(3):
        hs[b, pl.ds(0, WS), :] = jnp.zeros((WS, C), BF16)
        hs[b, pl.ds(WS + HW, WS), :] = jnp.zeros((WS, C), BF16)
    with scope("load"):
        for copy in loads:
            copy.wait()
        for copy in mine:
            copy.wait()
    savt[...] = savv[...].T
    latt[...] = latv[...].T

    def hidden(f):
        total = None
        for k in range(KT):
            moved = opad[block(f + KT - 1 - k), :]
            term = nt(moved, twv[k])
            total = term if total is None else total + term
        value = total.astype(BF16)
        hsend[block(f), :] = value
        return value

    def landing(n):
        return hs.at[1, block(n, WS), my_cols]

    xcopies = []
    arrived = 0
    for k in range(F - U):
        f = frame(k)
        with scope(f"owait{k}"):
            while arrived < k + 2:
                ocopies[arrived].wait()
                arrived += 1
        with scope(f"hidden{k}"):
            hidden(f)
        slot = lax.rem(f + me_c, 2)
        copy = pltpu.make_async_remote_copy(
            src_ref=hsend.at[block(f)], dst_ref=landing(me_s),
            send_sem=xsend.at[k], recv_sem=xrecv.at[slot],
            device_id=(me_z, f, me_t), device_id_type=MESH,
        )
        copy.start()
        xcopies.append(copy)
    with scope("owait"):
        while arrived < F:
            ocopies[arrived].wait()
            arrived += 1
    with scope("hiddensib"):
        hidden(sib)
    bcopies = [
        pltpu.make_async_remote_copy(
            src_ref=hsend.at[block(sib)], dst_ref=landing(me_s),
            send_sem=bsend.at[n], recv_sem=brecv.at[n],
            device_id=(me_z, sib, t), device_id_type=MESH,
        )
        for n, t in enumerate((1 - me_t, me_t))
    ]
    for copy in bcopies:
        copy.start()
    with scope("hiddenme"):
        value = hidden(me_s)
    ycopies = [
        pltpu.make_async_remote_copy(
            src_ref=hsend.at[block(me_s)], dst_ref=landing(me_s),
            send_sem=ysend.at[0], recv_sem=yrecv.at[0], device_id=mate, device_id_type=MESH,
        )
    ]
    ycopies[0].start()
    hs[1, block(me_s, WS), my_cols] = value

    with scope("relay"):
        for slot in range(2):
            src = far + (me_c if slot == 0 else 1 - me_c)
            pltpu.make_async_remote_copy(
                src_ref=hsend.at[block(me_s)], dst_ref=landing(src),
                send_sem=xsend.at[slot], recv_sem=xrecv.at[slot],
                device_id=(me_z, src, me_t), device_id_type=MESH,
            ).wait_recv()
            copy = pltpu.make_async_remote_copy(
                src_ref=landing(src), dst_ref=landing(src),
                send_sem=ysend.at[1 + slot], recv_sem=yrecv.at[1 + slot], device_id=mate, device_id_type=MESH,
            )
            copy.start()
            ycopies.append(copy)

    sent = {}

    def view(n):
        tap, at, rows = chunks[n]
        return tap, pl.ds(at, rows)

    def start1(n):
        tap, rows = view(n)
        copy = pltpu.make_async_remote_copy(
            src_ref=gsend.at[1 - me_c, :, tap, rows], dst_ref=g1.at[:, tap, rows],
            send_sem=s1s.at[n], recv_sem=s1r.at[n],
            device_id=(me_z, sib, me_t), device_id_type=MESH,
        )
        copy.start()
        sent[1, n] = copy

    def step1(n):
        tap, rows = view(n)
        sent[1, n].wait()
        other = 1 - me_u
        g2s[tap, rows] = (gsend[me_c, other, tap, rows].astype(F32) + g1[other, tap, rows].astype(F32)).astype(BF16)
        copy = pltpu.make_async_remote_copy(
            src_ref=g2s.at[tap, rows], dst_ref=g2r.at[tap, rows],
            send_sem=s2s.at[n], recv_sem=s2r.at[n],
            device_id=(me_z, far + me_c, me_t), device_id_type=MESH,
        )
        copy.start()
        sent[2, n] = copy

    half = Z // 2
    low = me_z < half
    is_end = jnp.logical_or(me_z == 0, me_z == Z - 1)
    is_inner = jnp.logical_or(me_z == half - 1, me_z == half)
    z_in = jnp.where(low, me_z + 1, me_z - 1)
    z_out = jnp.clip(jnp.where(low, me_z - 1, me_z + 1), 0, Z - 1)
    Z_INNER, Z_OUTER = 0, 1

    def hop(n, src, slot, target):
        tap, rows = view(n)
        return pltpu.make_async_remote_copy(
            src_ref=src.at[tap, rows], dst_ref=gzr.at[slot, tap, rows],
            send_sem=s3s.at[slot, n], recv_sem=s3r.at[slot, n],
            device_id=(target, me_s, me_t), device_id_type=MESH,
        )

    def to_inner(n):
        return hop(n, gz, Z_OUTER, z_in)

    def across(n):
        return hop(n, gz, Z_INNER, z_in)

    def to_outer(n):
        return hop(n, gf, Z_INNER, z_out)

    def step2(n):
        tap, rows = view(n)
        sent[2, n].wait()
        total = gsend[me_c, me_u, tap, rows].astype(F32) + g1[me_u, tap, rows].astype(F32)
        total = total + g2r[tap, rows].astype(F32)
        gzf[tap, rows] = total

        @pl.when(is_end)
        def _():
            gz[tap, rows] = total.astype(BF16)
            to_inner(n).start()

    def step3(n):
        tap, rows = view(n)

        @pl.when(is_inner)
        def _():
            to_inner(n).wait_recv()
            gz[tap, rows] = (gzf[tap, rows] + gzr[Z_OUTER, tap, rows].astype(F32)).astype(BF16)
            across(n).start()

    def step4(n):
        tap, rows = view(n)

        @pl.when(is_inner)
        def _():
            across(n).wait_recv()
            gf[tap, rows] = (gz[tap, rows].astype(F32) + gzr[Z_INNER, tap, rows].astype(F32)).astype(BF16)
            to_outer(n).start()

    def step5(n):
        tap, rows = view(n)

        @pl.when(is_end)
        def _():
            across(n).wait_recv()
            gf[tap, rows] = gzr[Z_INNER, tap, rows]

    def finish(n):
        @pl.when(is_inner)
        def _():
            across(n).wait_send()
            to_outer(n).wait_send()

        @pl.when(is_end)
        def _():
            to_inner(n).wait_send()

    def moved_at(tap):
        row, col = tap // 3, tap % 3
        return hs[col, pl.ds((2 - row) * WS, HW), :]

    def gradient(tap):
        if tap < KT:
            part = nn(savt[...], opad[pl.ds((KT - 1 - tap) * Pl, F * Pl), :])
        else:
            part = nn(latt[...], moved_at(tap - KT))
        for s in range(S):
            gsend[s % 2, s // 2, tap] = part[:, s * Cs : (s + 1) * Cs].astype(BF16)
        for n, chunk in enumerate(chunks):
            if chunk[0] == tap:
                start1(n)

    def arrive():
        for copy in ycopies + bcopies:
            copy.wait()
        for copy in xcopies:
            copy.wait_send()

    tile = 4 * WS

    def shift():
        for r in range(0, HW, tile):
            hwide[pl.ds(8 + r, tile), :] = hs[1, pl.ds(WS + r, tile), :].astype(F32)
        column = lax.rem(lax.broadcasted_iota(jnp.int32, (tile, C), 0), WS)
        for b in (-1, 1):
            keep = column != (0 if b == 1 else WS - 1)
            for r in range(0, HW, tile):
                value = hwide[pl.ds(8 + r - b, tile), :]
                hs[b + 1, pl.ds(WS + r, tile), :] = jnp.where(keep, value, 0.0).astype(BF16)

    images = [3 * row + col for col in (1, 0, 2) for row in range(3)]

    def image(n):
        term = nt(moved_at(images[n]), swv[images[n]])
        if n == 0:
            acc[...] = term
        elif n < len(images) - 1:
            acc[...] += term
        else:
            ig[...] = (acc[...] + term).astype(BF16)

    steps = {1: step1, 2: step2, 3: step3, 4: step4, 5: step5, "g": gradient, "i": image}
    for kind, n in order(chunks, KT, len(images), Cl):
        with scope(f"{kind}_{n}"):
            if kind == "h":
                arrive()
            elif kind == "s":
                shift()
            else:
                steps[kind](n)
    with scope("fin"):
        for n in range(len(chunks)):
            finish(n)


def fused(sizes, latents, saved_input, out_grad, temporal_weight, spatial_weight):
    S, T, Z = sizes
    F, Pl, Cl = out_grad.shape[1:]
    KT, _, C = temporal_weight.shape
    taps = KT + spatial_weight.shape[0]
    HW = latents.shape[2]
    Cs = C // S
    U = S // 2
    scale = 1.0 / math.sqrt(Z * F * HS * WS)
    spatial = [KT + 3 * row + col for col in (1, 0, 2) for row in range(3)]
    chunks = pieces_of(list(range(KT)) + spatial, [1] * KT + PARTS, Cl)
    N = len(chunks)
    dims = (S, T, Z, F, Pl, Cl, Cs, chunks, KT)
    V = pltpu.VMEM
    D = pltpu.SemaphoreType.DMA
    hbm = pl.BlockSpec(memory_space=pltpu.HBM)
    vmem = pl.BlockSpec(memory_space=pltpu.VMEM)
    ig, sums = pl.pallas_call(
        functools.partial(kernel, dims),
        out_shape=(
            jax.ShapeDtypeStruct((HW, Cl), BF16),
            jax.ShapeDtypeStruct((taps, Cl, Cs), BF16),
        ),
        in_specs=[hbm] * 5,
        out_specs=(vmem,) * 2,
        scratch_shapes=[
            V((HW, Cl), BF16), V((F * Pl, Cl), BF16), V((KT, Cl, C), BF16), V((taps - KT, Cl, C), BF16),
            V(((F + 2) * Pl, C), BF16), V((F * Pl, Cl), BF16),
            V((HW + 16, C), F32), V((3, HW + 2 * WS, C), BF16),
            V((Cl, F * Pl), BF16), V((Cl, HW), BF16), V((HW, Cl), F32),
            V((2, U, taps, Cl, Cs), BF16), V((U, taps, Cl, Cs), BF16), V((taps, Cl, Cs), BF16),
            V((taps, Cl, Cs), BF16), V((taps, Cl, Cs), BF16), V((taps, Cl, Cs), F32), V((2, taps, Cl, Cs), BF16),
            D((4,)), D((F,)), D((F,)), D((F,)), D((2,)), D((2,)), D((2,)), D((2,)), D((3,)), D((3,)),
            D((N,)), D((N,)), D((N,)), D((N,)),
            D((2, N)), D((2, N)),
        ],
        compiler_params=pltpu.CompilerParams(
            collective_id=0, has_side_effects=True, vmem_limit_bytes=34 * 2**20
        ),
    )(*(
        pltpu.with_memory_space_constraint(value, pltpu.HBM)
        for value in (
            latents.reshape(HW, Cl), saved_input.reshape(F * Pl, Cl), out_grad.reshape(F * Pl, Cl),
            temporal_weight, spatial_weight,
        )
    ))

    def finish(ig_ref, sums_ref, ig_out, tg_out, sg_out):
        ig_out[...] = ig_ref[...]
        tg_out[...] = sums_ref[:KT].astype(F32) * scale
        sg_out[...] = sums_ref[KT:].astype(F32) * scale

    ig, tg, sg = pl.pallas_call(
        finish,
        out_shape=(
            jax.ShapeDtypeStruct((HW, Cl), BF16),
            jax.ShapeDtypeStruct((KT, Cl, Cs), F32),
            jax.ShapeDtypeStruct((taps - KT, Cl, Cs), F32),
        ),
        in_specs=[vmem] * 2,
        out_specs=(vmem,) * 3,
        compiler_params=pltpu.CompilerParams(vmem_limit_bytes=16 * 2**20),
    )(ig, sums)
    return ig.reshape(latents.shape), tg, sg


def plain(latents, saved_input, out_grad, temporal_weight, spatial_weight):
    clips_all = latents.shape[0] * lax.axis_size("clip")
    frames_all = latents.shape[1] * lax.axis_size("sp")
    scale_factor = 1.0 / math.sqrt(clips_all * frames_all * HS * WS)
    frames_count = out_grad.shape[1]
    local_in = temporal_weight.shape[1]
    saved_padded = pad_frames(saved_input)
    block_in = lax.all_gather(out_grad, "tp", axis=3, tiled=True)
    padded = pad_frames(block_in)
    hidden_acc = jnp.zeros(out_grad.shape[:3] + (local_in,), F32)
    parts = []
    for tap_index in range(3):
        shifted = padded[:, 2 - tap_index : 2 - tap_index + frames_count]
        hidden_acc = hidden_acc + jnp.einsum(
            "bfpo,io->bfpi", shifted, temporal_weight[tap_index], preferred_element_type=F32
        )
        window = saved_padded[:, tap_index : tap_index + frames_count]
        parts.append(jnp.einsum("bfpi,bfpo->io", window, block_in, preferred_element_type=F32))
    temporal_local = jnp.stack(parts)
    hidden_grad = hidden_acc.astype(BF16)
    regrouped = lax.all_to_all(hidden_grad, "sp", split_axis=1, concat_axis=2, tiled=True)
    batch = latents.shape[0] * latents.shape[1]
    image_pad = jnp.pad(latents.reshape(batch, HS, WS, local_in), ((0, 0), (1, 1), (1, 1), (0, 0)))
    block_in = lax.all_gather(regrouped, "tp", axis=3, tiled=True)
    whole = block_in.reshape(batch, HS, WS, block_in.shape[3])
    grid = jnp.pad(whole, ((0, 0), (1, 1), (1, 1), (0, 0)))
    input_acc = jnp.zeros((batch, HS, WS, local_in), F32)
    parts = []
    for row in (-1, 0, 1):
        for col in (-1, 0, 1):
            tap_index = 3 * (row + 1) + (col + 1)
            moved = grid[:, 1 - row : 1 - row + HS, 1 - col : 1 - col + WS]
            input_acc = input_acc + jnp.einsum(
                "gabo,co->gabc", moved, spatial_weight[tap_index], preferred_element_type=F32
            )
            window = image_pad[:, 1 + row : 1 + row + HS, 1 + col : 1 + col + WS]
            parts.append(jnp.einsum("gabc,gabo->co", window, whole, preferred_element_type=F32))
    spatial_local = jnp.stack(parts)
    input_grad = input_acc.reshape(latents.shape).astype(BF16)
    temporal_grad, spatial_grad = lax.psum(
        tuple(
            lax.psum_scatter(value * scale_factor, "sp", scatter_dimension=2, tiled=True)
            for value in (temporal_local, spatial_local)
        ),
        "clip",
    )
    return input_grad, temporal_grad, spatial_grad


PARTS = [2, 1, 1, 1, 1, 1, 2, 2, 2]


def solution(mesh):
    sizes = (mesh.shape["sp"], mesh.shape["tp"], mesh.shape["clip"])

    def local(latents, saved_input, out_grad, temporal_weight, spatial_weight):
        S, T, Z = sizes
        cols = temporal_weight.shape[2] // S
        fits = (
            latents.shape[:2] == (1, 1) and S == out_grad.shape[1] == 4 and T == 2 and Z == 4
            and cols % 128 == 0 and out_grad.shape[3] % 128 == 0 and out_grad.shape[2] % WS == 0
        )
        args = (latents, saved_input, out_grad, temporal_weight, spatial_weight)
        return fused(sizes, *args) if fits else plain(*args)

    return jax.shard_map(
        local,
        mesh=mesh,
        in_specs=(
            P("clip", "sp", None, "tp"),
            P("clip", None, "sp", "tp"),
            P("clip", None, "sp", "tp"),
            P(None, "tp", None),
            P(None, "tp", None),
        ),
        out_specs=(P("clip", "sp", None, "tp"), P(None, "tp", "sp"), P(None, "tp", "sp")),
        check_vma=False,
    )
```

```python
import contextlib
import functools
import math

import jax
import jax.numpy as jnp
from jax import lax
from jax.experimental import pallas as pl
from jax.experimental.pallas import tpu as pltpu
from jax.sharding import PartitionSpec as P

HS = 32
WS = 32
MESH = pl.DeviceIdType.MESH
F32 = jnp.float32
BF16 = jnp.bfloat16


def pad_frames(values):
    return jnp.pad(values, ((0, 0), (1, 1), (0, 0), (0, 0)))


def nt(a, b):
    return lax.dot_general(a, b, (((1,), (1,)), ((), ())), preferred_element_type=F32)


def nn(a, b):
    return lax.dot_general(a, b, (((1,), (0,)), ((), ())), preferred_element_type=F32)


scope = contextlib.nullcontext


def pieces_of(taps, parts, rows):
    return [(tap, part * (rows // n), rows // n) for tap, n in zip(taps, parts) for part in range(n)]


def order(chunks, first, images, rows):
    hop, core_hop, link, core = 1.8, 0.65, 1.39, 0.44
    arrival = 3.0
    now, free = -2.0, {"core": 0.0, "x": -2.0, "z": 0.0, "across": 0.0, "back": 0.0}
    pending, out = {}, []

    def send(name, n, step):
        part = chunks[n][2] / rows
        free[name] = max(free[name], now) + (core if name == "core" else link) * part
        pending[step, n] = free[name] + (core_hop if name == "core" else hop)

    taps = list(dict.fromkeys(tap for tap, _, _ in chunks))
    late, filler = taps[first:], ["h", "s"] + list(range(images))
    for n, chunk in enumerate(chunks):
        if chunk[0] in taps[:first]:
            send("x", n, 2)
    now = 0.0
    while pending or late or filler:
        ready = sorted((at, key) for key, at in pending.items() if at <= now)
        if ready:
            at, (step, n) = ready[0]
            now += 0.06 * chunks[n][2] / rows
            del pending[step, n]
            out.append((step, n))
            if step < 5:
                send(("core", "x", "z", "across", "back")[step], n, step + 1)
            continue
        soon = min(pending.values()) if pending else 1e9
        if late:
            tap = late.pop(0)
            out.append(("g", tap))
            now += 0.45
            for n, chunk in enumerate(chunks):
                if chunk[0] == tap:
                    send("core", n, 1)
        elif filler and now >= arrival and (soon > now + 0.25 or not pending):
            kind = filler.pop(0)
            out.append((kind, 0) if isinstance(kind, str) else ("i", kind))
            now += 0.1 if kind == "h" else 0.58
        else:
            now = max(now, soon if not filler or now >= arrival else min(soon, arrival))
    return out


def kernel(
    dims, lat, sav, og, tw, sw, ig, gf,
    savv, twv, twx, swv, opad, hid, savt, latl, lwide, latt, hwide, hs, acc,
    gsend, g1, g2s, g2r, gz, gzf, gzr,
    lsem, osend, orecv, osem, xsend, xrecv, bsem, ysend, yrecv,
    lxsend, lxrecv, wysem, wzsend, wzrecv, wcsend, wcrecv,
    s1s, s1r, s2s, s2r, s3s, s3r,
):
    S, T, Z, F, Pl, Cl, Cs, chunks, KT = dims
    U = S // 2
    HW = S * Pl
    C = T * Cl
    R = Pl // WS
    me_s, me_t, me_z = lax.axis_index("sp"), lax.axis_index("tp"), lax.axis_index("clip")
    me_u, me_c = me_s // 2, lax.rem(me_s, 2)
    sib = me_u * 2 + 1 - me_c
    far = (1 - me_u) * 2
    mate = (me_z, me_s, 1 - me_t)
    near = (me_z, sib, me_t)
    others = (sib, far + me_c, far + 1 - me_c)

    def remote(src, dst, send, recv, device):
        return pltpu.make_async_remote_copy(
            src_ref=src, dst_ref=dst, send_sem=send, recv_sem=recv, device_id=device, device_id_type=MESH
        )

    def block(n, base=0):
        return pl.ds(pl.multiple_of(base + n * Pl, 16), Pl)

    def window(n):
        at = jnp.clip(n * R - 1, 0, HW // WS - R - 2)
        return (
            pl.ds(pl.multiple_of(at * WS, WS), (R + 2) * WS),
            pl.ds(pl.multiple_of((at - n * R + 2) * WS, WS), (R + 2) * WS),
        )

    my_cols = pl.ds(pl.multiple_of(me_t * Cl, Cl), Cl)
    mate_cols = pl.ds(pl.multiple_of((1 - me_t) * Cl, Cl), Cl)
    loads = [
        pltpu.make_async_copy(src, dst, lsem.at[n]) for n, (src, dst) in enumerate(((tw, twv), (sav, savv), (sw, swv)))
    ]
    mine = [
        pltpu.make_async_copy(og.at[pl.ds(f * Pl, Pl)], opad.at[pl.ds((f + 1) * Pl, Pl), my_cols], osem.at[f])
        for f in range(F)
    ]
    for f in range(F):
        latl[f, pl.ds(WS, WS), :] = jnp.zeros((WS, Cl), BF16)
        latl[f, pl.ds((R + 2) * WS, WS), :] = jnp.zeros((WS, Cl), BF16)
    for copy in mine + loads:
        copy.start()

    with scope("barrier"):
        barrier = pltpu.get_barrier_semaphore()
        peers = [mate, near, (me_z, others[1], me_t), (me_z, others[2], me_t)]
        count = len(peers) + Z - 1
        for peer in peers:
            pl.semaphore_signal(barrier, inc=1, device_id=peer, device_id_type=MESH)
        for dz in range(1, Z):
            pl.semaphore_signal(
                barrier, inc=1, device_id=(lax.rem(me_z + dz, Z), me_s, me_t), device_id_type=MESH
            )
        pl.semaphore_wait(barrier, count)

    def frame(k):
        return jnp.where(me_u == 0, F - 1 - k, k)

    share = Cl // (2 * Z)

    def slice_of(z, c):
        return pl.ds(pl.multiple_of((z * 2 + c) * share, 16), share)

    here = slice_of(me_z, me_c)
    wy = remote(tw.at[:, here], twx.at[:, here], wysem.at[0], wysem.at[1], mate)
    wy.start()
    ocopies = []
    for k in range(F):
        f = frame(k)
        copy = remote(og.at[block(f)], opad.at[block(f, Pl), my_cols], osend.at[k], orecv.at[k], mate)
        copy.start()
        ocopies.append(copy)
    lcopies = []
    for n in (1, 2, 0):
        src, dst = window(others[n])
        copy = remote(lat.at[src], latl.at[me_s, dst], lxsend.at[n], lxrecv.at[n], (me_z, others[n], me_t))
        copy.start()
        lcopies.append(copy)
    src, dst = window(me_s)
    own = pltpu.make_async_copy(lat.at[src], latl.at[me_s, dst], lsem.at[3])
    own.start()

    opad[pl.ds(0, Pl), :] = jnp.zeros((Pl, C), BF16)
    opad[pl.ds((F + 1) * Pl, Pl), :] = jnp.zeros((Pl, C), BF16)
    hwide[pl.ds(0, 8), :] = jnp.zeros((8, C), F32)
    hwide[pl.ds(8 + HW, 8), :] = jnp.zeros((8, C), F32)
    for b in range(3):
        hs[b, pl.ds(0, WS), :] = jnp.zeros((WS, C), BF16)
        hs[b, pl.ds(WS + HW, WS), :] = jnp.zeros((WS, C), BF16)
    with scope("load"):
        for copy in mine + loads:
            copy.wait()
    savt[...] = savv[...].T

    with scope("wy"):
        wy.wait()
    part = twx.at[:, here]
    wcopies = [remote(part, part, wcsend.at[0], wcrecv.at[0], near)]
    wcopies[0].start()
    wzcopies = []
    for dz in range(1, Z):
        copy = remote(
            part, part, wzsend.at[dz - 1], wzrecv.at[dz - 1], (lax.rem(me_z + dz, Z), me_s, me_t)
        )
        copy.start()
        wzcopies.append(copy)

    def pass_on(dz):
        wzcopies[dz - 1].wait_recv()
        piece = twx.at[:, slice_of(lax.rem(me_z + Z - dz, Z), me_c)]
        copy = remote(piece, piece, wcsend.at[dz], wcrecv.at[dz], near)
        copy.start()
        wcopies.append(copy)

    with scope("lwait"):
        own.wait()
        for copy in lcopies:
            copy.wait()
    span = (R + 2) * WS
    column = lax.rem(lax.broadcasted_iota(jnp.int32, (span, Cl), 0), WS)

    def latents_of(f):
        lwide[...] = latl[f].astype(F32)
        for b in range(3):
            if b == 1:
                value = latl[f, pl.ds(WS, span), :]
            else:
                value = lwide[pl.ds(WS + b - 1, span), :]
                value = jnp.where(column != (WS - 1 if b == 2 else 0), value, 0.0).astype(BF16)
            for row in range(3):
                latt[3 * row + b, :, pl.ds(f * Pl, Pl)] = value[row * WS : row * WS + Pl].T

    def landing(n):
        return hs.at[1, block(n, WS), my_cols]

    def hidden(weights, at, size):
        total = None
        for k in range(KT):
            term = nt(opad[pl.ds(pl.multiple_of(at + (KT - 1 - k) * Pl, 16), size), :], weights[k])
            total = term if total is None else total + term
        return total.astype(BF16)

    xcopies = []
    arrived = 0

    def take(n):
        nonlocal arrived
        with scope(f"owait{n}"):
            while arrived < n:
                ocopies[arrived].wait()
                arrived += 1

    for k in range(F - U):
        f = frame(k)
        with scope(f"lshift{k}"):
            for part_f in range(k * U, (k + 1) * U):
                latents_of(part_f)
        take(k + 2)
        with scope(f"hidden{k}"):
            hid[block(f), my_cols] = hidden(twv, f * Pl, Pl)
        copy = remote(
            hid.at[block(f), my_cols], landing(me_s), xsend.at[k], xrecv.at[lax.rem(f + me_c, 2)], (me_z, f, me_t)
        )
        copy.start()
        xcopies.append(copy)
        with scope(f"pass{k}"):
            pass_on(1 if k == 0 else Z - 1)
    take(F)

    sent = {}

    def view(n):
        tap, at, rows = chunks[n]
        return tap, pl.ds(at, rows)

    def start1(n):
        at = view(n)
        sent[1, n] = remote(gsend.at[(1 - me_c, slice(None)) + at], g1.at[(slice(None),) + at], s1s.at[n], s1r.at[n], near)
        sent[1, n].start()

    def step1(n):
        at = view(n)
        sent[1, n].wait()
        other = 1 - me_u
        g2s[at] = (gsend[(me_c, other) + at].astype(F32) + g1[(other,) + at].astype(F32)).astype(BF16)
        sent[2, n] = remote(g2s.at[at], g2r.at[at], s2s.at[n], s2r.at[n], (me_z, others[1], me_t))
        sent[2, n].start()

    half = Z // 2
    low = me_z < half
    is_end = jnp.logical_or(me_z == 0, me_z == Z - 1)
    is_inner = jnp.logical_or(me_z == half - 1, me_z == half)
    z_in = jnp.where(low, me_z + 1, me_z - 1)
    z_out = jnp.clip(jnp.where(low, me_z - 1, me_z + 1), 0, Z - 1)
    Z_INNER, Z_OUTER = 0, 1

    def hop(n, src, slot, target):
        at = view(n)
        return remote(src.at[at], gzr.at[(slot,) + at], s3s.at[slot, n], s3r.at[slot, n], (target, me_s, me_t))

    def to_inner(n):
        return hop(n, gz, Z_OUTER, z_in)

    def across(n):
        return hop(n, gz, Z_INNER, z_in)

    def to_outer(n):
        return hop(n, gf, Z_INNER, z_out)

    def step2(n):
        at = view(n)
        sent[2, n].wait()
        total = gsend[(me_c, me_u) + at].astype(F32) + g1[(me_u,) + at].astype(F32)
        total = total + g2r[at].astype(F32)
        gzf[at] = total

        @pl.when(is_end)
        def _():
            gz[at] = total.astype(BF16)
            to_inner(n).start()

    def step3(n):
        at = view(n)

        @pl.when(is_inner)
        def _():
            to_inner(n).wait_recv()
            gz[at] = (gzf[at] + gzr[(Z_OUTER,) + at].astype(F32)).astype(BF16)
            across(n).start()

    def step4(n):
        at = view(n)

        @pl.when(is_inner)
        def _():
            across(n).wait_recv()
            value = (gz[at].astype(F32) + gzr[(Z_INNER,) + at].astype(F32)).astype(BF16)
            gf[at] = value
            to_outer(n).start()

    def step5(n):
        at = view(n)

        @pl.when(is_end)
        def _():
            across(n).wait_recv()
            gf[at] = gzr[(Z_INNER,) + at]

    def finish(n):
        @pl.when(is_inner)
        def _():
            across(n).wait_send()
            to_outer(n).wait_send()

        @pl.when(is_end)
        def _():
            to_inner(n).wait_send()

    def gradient(tap):
        if tap < KT:
            part = nn(savt[...], opad[pl.ds((KT - 1 - tap) * Pl, F * Pl), :])
        else:
            part = nn(latt[tap - KT], hid[...])
        for s in range(S):
            gsend[s % 2, s // 2, tap] = part[:, s * Cs : (s + 1) * Cs].astype(BF16)
        for n, chunk in enumerate(chunks):
            if chunk[0] == tap:
                start1(n)

    early = [n for n, chunk in enumerate(chunks) if chunk[0] < KT]
    for tap in range(KT):
        with scope(f"g_{tap}"):
            gradient(tap)
    with scope("passlast"):
        for dz in range(2, Z - 1):
            pass_on(dz)
    with scope("early0"):
        step1(early[0])
    with scope("hiddenown"):
        for k in range(F - U, F):
            f = frame(k)
            hid[block(f), my_cols] = hidden(twv, f * Pl, Pl)
    with scope("early"):
        for n in early[1:]:
            step1(n)
    with scope("wwait"):
        for copy in wcopies:
            copy.wait()
        for copy in wzcopies:
            copy.wait_send()
    with scope("hiddenrest"):
        hid[:, mate_cols] = hidden(twx, 0, F * Pl)
    to_sib = remote(hid.at[block(sib)], hs.at[1, block(me_s, WS)], bsem.at[0], bsem.at[1], near)
    to_sib.start()
    ycopies = []
    with scope("relay"):
        for slot in range(2):
            source = others[1 + slot]
            remote(
                landing(source), landing(source), xsend.at[slot], xrecv.at[slot], (me_z, source, me_t)
            ).wait_recv()
            copy = remote(landing(source), landing(source), ysend.at[slot], yrecv.at[slot], mate)
            copy.start()
            ycopies.append(copy)

    def arrive():
        to_sib.wait()
        for copy in ycopies:
            copy.wait()
        for copy in xcopies:
            copy.wait_send()
        hs[1, block(me_s, WS), :] = hid[block(me_s), :]

    tile = 4 * WS

    def shift():
        for r in range(0, HW, tile):
            hwide[pl.ds(8 + r, tile), :] = hs[1, pl.ds(WS + r, tile), :].astype(F32)
        column = lax.rem(lax.broadcasted_iota(jnp.int32, (tile, C), 0), WS)
        for b in (-1, 1):
            keep = column != (0 if b == 1 else WS - 1)
            for r in range(0, HW, tile):
                value = hwide[pl.ds(8 + r - b, tile), :]
                hs[b + 1, pl.ds(WS + r, tile), :] = jnp.where(keep, value, 0.0).astype(BF16)

    images = swv.shape[0]

    def image(tap):
        row, col = tap // 3, tap % 3
        term = nt(hs[col, pl.ds((2 - row) * WS, HW), :], swv[tap])
        if tap == 0:
            acc[...] = term
        elif tap < images - 1:
            acc[...] += term
        else:
            ig[...] = (acc[...] + term).astype(BF16)

    steps = {1: step1, 2: step2, 3: step3, 4: step4, 5: step5, "g": gradient, "i": image}
    for kind, n in order(chunks, KT, images, Cl):
        with scope(f"{kind}_{n}"):
            if kind == "h":
                arrive()
            elif kind == "s":
                shift()
            else:
                steps[kind](n)
    with scope("fin"):
        for n in range(len(chunks)):
            finish(n)


def fused(sizes, latents, saved_input, out_grad, temporal_weight, spatial_weight):
    S, T, Z = sizes
    F, Pl, Cl = out_grad.shape[1:]
    KT, _, C = temporal_weight.shape
    taps = KT + spatial_weight.shape[0]
    HW = latents.shape[2]
    Cs = C // S
    U = S // 2
    scale = 1.0 / math.sqrt(Z * F * HS * WS)
    chunks = pieces_of(list(range(taps)), [1] * KT + PARTS, Cl)
    N = len(chunks)
    dims = (S, T, Z, F, Pl, Cl, Cs, chunks, KT)
    V = pltpu.VMEM
    D = pltpu.SemaphoreType.DMA
    hbm = pl.BlockSpec(memory_space=pltpu.HBM)
    vmem = pl.BlockSpec(memory_space=pltpu.VMEM)
    ig, sums = pl.pallas_call(
        functools.partial(kernel, dims),
        out_shape=(
            jax.ShapeDtypeStruct((HW, Cl), BF16),
            jax.ShapeDtypeStruct((taps, Cl, Cs), BF16),
        ),
        in_specs=[hbm] * 5,
        out_specs=(vmem,) * 2,
        scratch_shapes=[
            V((F * Pl, Cl), BF16), V((KT, Cl, C), BF16), V((KT, Cl, C), BF16), V((taps - KT, Cl, C), BF16),
            V(((F + 2) * Pl, C), BF16), V((F * Pl, C), BF16), V((Cl, F * Pl), BF16),
            V((F, Pl + 4 * WS, Cl), BF16), V((Pl + 4 * WS, Cl), F32), V((taps - KT, Cl, F * Pl), BF16),
            V((HW + 16, C), F32), V((3, HW + 2 * WS, C), BF16), V((HW, Cl), F32),
            V((2, U, taps, Cl, Cs), BF16), V((U, taps, Cl, Cs), BF16), V((taps, Cl, Cs), BF16),
            V((taps, Cl, Cs), BF16), V((taps, Cl, Cs), BF16), V((taps, Cl, Cs), F32), V((2, taps, Cl, Cs), BF16),
            D((4,)), D((F,)), D((F,)), D((F,)), D((U,)), D((U,)), D((2,)), D((2,)), D((2,)),
            D((3,)), D((3,)), D((2,)), D((Z - 1,)), D((Z - 1,)), D((Z,)), D((Z,)),
            D((N,)), D((N,)), D((N,)), D((N,)),
            D((2, N)), D((2, N)),
        ],
        compiler_params=pltpu.CompilerParams(
            collective_id=0, has_side_effects=True, vmem_limit_bytes=40 * 2**20
        ),
    )(*(
        pltpu.with_memory_space_constraint(value, pltpu.HBM)
        for value in (
            latents.reshape(HW, Cl), saved_input.reshape(F * Pl, Cl), out_grad.reshape(F * Pl, Cl),
            temporal_weight, spatial_weight,
        )
    ))

    def finish(ig_ref, sums_ref, ig_out, tg_out, sg_out):
        ig_out[...] = ig_ref[...]
        tg_out[...] = sums_ref[:KT].astype(F32) * scale
        sg_out[...] = sums_ref[KT:].astype(F32) * scale

    ig, tg, sg = pl.pallas_call(
        finish,
        out_shape=(
            jax.ShapeDtypeStruct((HW, Cl), BF16),
            jax.ShapeDtypeStruct((KT, Cl, Cs), F32),
            jax.ShapeDtypeStruct((taps - KT, Cl, Cs), F32),
        ),
        in_specs=[vmem] * 2,
        out_specs=(vmem,) * 3,
        compiler_params=pltpu.CompilerParams(vmem_limit_bytes=16 * 2**20),
    )(ig, sums)
    return ig.reshape(latents.shape), tg, sg


def plain(latents, saved_input, out_grad, temporal_weight, spatial_weight):
    clips_all = latents.shape[0] * lax.axis_size("clip")
    frames_all = latents.shape[1] * lax.axis_size("sp")
    scale_factor = 1.0 / math.sqrt(clips_all * frames_all * HS * WS)
    frames_count = out_grad.shape[1]
    local_in = temporal_weight.shape[1]
    saved_padded = pad_frames(saved_input)
    block_in = lax.all_gather(out_grad, "tp", axis=3, tiled=True)
    padded = pad_frames(block_in)
    hidden_acc = jnp.zeros(out_grad.shape[:3] + (local_in,), F32)
    parts = []
    for tap_index in range(3):
        shifted = padded[:, 2 - tap_index : 2 - tap_index + frames_count]
        hidden_acc = hidden_acc + jnp.einsum(
            "bfpo,io->bfpi", shifted, temporal_weight[tap_index], preferred_element_type=F32
        )
        window = saved_padded[:, tap_index : tap_index + frames_count]
        parts.append(jnp.einsum("bfpi,bfpo->io", window, block_in, preferred_element_type=F32))
    temporal_local = jnp.stack(parts)
    hidden_grad = hidden_acc.astype(BF16)
    regrouped = lax.all_to_all(hidden_grad, "sp", split_axis=1, concat_axis=2, tiled=True)
    batch = latents.shape[0] * latents.shape[1]
    image_pad = jnp.pad(latents.reshape(batch, HS, WS, local_in), ((0, 0), (1, 1), (1, 1), (0, 0)))
    block_in = lax.all_gather(regrouped, "tp", axis=3, tiled=True)
    whole = block_in.reshape(batch, HS, WS, block_in.shape[3])
    grid = jnp.pad(whole, ((0, 0), (1, 1), (1, 1), (0, 0)))
    input_acc = jnp.zeros((batch, HS, WS, local_in), F32)
    parts = []
    for row in (-1, 0, 1):
        for col in (-1, 0, 1):
            tap_index = 3 * (row + 1) + (col + 1)
            moved = grid[:, 1 - row : 1 - row + HS, 1 - col : 1 - col + WS]
            input_acc = input_acc + jnp.einsum(
                "gabo,co->gabc", moved, spatial_weight[tap_index], preferred_element_type=F32
            )
            window = image_pad[:, 1 + row : 1 + row + HS, 1 + col : 1 + col + WS]
            parts.append(jnp.einsum("gabc,gabo->co", window, whole, preferred_element_type=F32))
    spatial_local = jnp.stack(parts)
    input_grad = input_acc.reshape(latents.shape).astype(BF16)
    temporal_grad, spatial_grad = lax.psum(
        tuple(
            lax.psum_scatter(value * scale_factor, "sp", scatter_dimension=2, tiled=True)
            for value in (temporal_local, spatial_local)
        ),
        "clip",
    )
    return input_grad, temporal_grad, spatial_grad


PARTS = [2, 1, 1, 1, 1, 1, 1, 2, 2]


def solution(mesh):
    sizes = (mesh.shape["sp"], mesh.shape["tp"], mesh.shape["clip"])

    def local(latents, saved_input, out_grad, temporal_weight, spatial_weight):
        S, T, Z = sizes
        cols = temporal_weight.shape[2] // S
        fits = (
            latents.shape[:2] == (1, 1) and S == out_grad.shape[1] == 4 and T == 2 and Z == 4
            and cols % 128 == 0 and out_grad.shape[3] % 256 == 0 and out_grad.shape[2] % 128 == 0
            and latents.shape[2] == HS * WS == S * out_grad.shape[2]
        )
        args = (latents, saved_input, out_grad, temporal_weight, spatial_weight)
        return fused(sizes, *args) if fits else plain(*args)

    return jax.shard_map(
        local,
        mesh=mesh,
        in_specs=(
            P("clip", "sp", None, "tp"),
            P("clip", None, "sp", "tp"),
            P("clip", None, "sp", "tp"),
            P(None, "tp", None),
            P(None, "tp", None),
        ),
        out_specs=(P("clip", "sp", None, "tp"), P(None, "tp", "sp"), P(None, "tp", "sp")),
        check_vma=False,
    )
```

```python
import contextlib
import functools
import math

import jax
import jax.numpy as jnp
from jax import lax
from jax.experimental import pallas as pl
from jax.experimental.pallas import tpu as pltpu
from jax.sharding import PartitionSpec as P

HS = 32
WS = 32
MESH = pl.DeviceIdType.MESH
F32 = jnp.float32
BF16 = jnp.bfloat16


def pad_frames(values):
    return jnp.pad(values, ((0, 0), (1, 1), (0, 0), (0, 0)))


def nt(a, b):
    return lax.dot_general(a, b, (((1,), (1,)), ((), ())), preferred_element_type=F32)


def nn(a, b):
    return lax.dot_general(a, b, (((1,), (0,)), ((), ())), preferred_element_type=F32)


scope = contextlib.nullcontext


def pieces_of(taps, parts, rows):
    return [(tap, part * (rows // n), rows // n) for tap, n in zip(taps, parts) for part in range(n)]


def order(chunks, first, images, rows):
    hop, core_hop, link, core = HOP, 0.65, 1.39, 0.44
    arrival = 8.0
    now, free = START, {"core": 0.0, "x": START, "z": 0.0, "across": 0.0, "back": 0.0}
    pending, out = {}, []

    def send(name, n, step):
        part = chunks[n][2] / rows
        free[name] = max(free[name], now) + (core if name == "core" else link) * part
        pending[step, n] = free[name] + (core_hop if name == "core" else hop)

    taps = list(dict.fromkeys(tap for tap, _, _ in chunks))
    late, filler = taps[first:], ["h", "s"] + list(range(images))
    for n, chunk in enumerate(chunks):
        if chunk[0] in taps[:first]:
            send("x", n, 2)
    now = 0.0
    while pending or late or filler:
        ready = sorted((at, key) for key, at in pending.items() if at <= now)
        if ready:
            at, (step, n) = ready[0]
            now += 0.06 * chunks[n][2] / rows
            del pending[step, n]
            out.append((step, n))
            if step < 5:
                send(("core", "x", "z", "across", "back")[step], n, step + 1)
            continue
        soon = min(pending.values()) if pending else 1e9
        if late:
            tap = late.pop(0)
            out.append(("g", tap))
            now += 0.7 if len(taps) - first - len(late) <= 3 else 0.45
            for n, chunk in enumerate(chunks):
                if chunk[0] == tap:
                    send("core", n, 1)
        elif filler and now >= arrival and (soon > now + 0.25 or not pending):
            kind = filler.pop(0)
            out.append((kind, 0) if isinstance(kind, str) else ("i", kind))
            now += 0.1 if kind == "h" else 0.55 if kind == "s" else 0.3
        else:
            now = max(now, soon if not filler or now >= arrival else min(soon, arrival))
    return out


def kernel(
    dims, lat, sav, og, tw, sw, ig_out, sums_out,
    savv, twv, twx, swv, opad, hid, savt, latl, lwide, latt, hwide, hs, acc, ig, gf, sums,
    gsend, g1, g2s, g2r, gz, gzf, gzr,
    lsem, osend, orecv, osem, xsend, xrecv, bsem, ysem, lxsem, wysem, wzsend, wzrecv, wxsend, wxrecv, wcsem,
    s1s, s1r, s2s, s2r, s3s, s3r, isem, rsem,
):
    S, T, Z, F, Pl, Cl, Cs, scale, chunks, KT = dims
    U = S // 2
    HW = S * Pl
    C = T * Cl
    R = Pl // WS
    me_s, me_t, me_z = lax.axis_index("sp"), lax.axis_index("tp"), lax.axis_index("clip")
    me_u, me_c = me_s // 2, lax.rem(me_s, 2)
    sib = me_u * 2 + 1 - me_c
    far = (1 - me_u) * 2
    mate = (me_z, me_s, 1 - me_t)
    near = (me_z, sib, me_t)
    others = (sib, far + me_c, far + 1 - me_c)

    def remote(src, dst, send, recv, device):
        return pltpu.make_async_remote_copy(
            src_ref=src, dst_ref=dst, send_sem=send, recv_sem=recv, device_id=device, device_id_type=MESH
        )

    def block(n, base=0):
        return pl.ds(pl.multiple_of(base + n * Pl, 16), Pl)

    def window(n):
        at = jnp.clip(n * R - 1, 0, HW // WS - R - 2)
        return (
            pl.ds(pl.multiple_of(at * WS, WS), (R + 2) * WS),
            pl.ds(pl.multiple_of((at - n * R + 2) * WS, WS), (R + 2) * WS),
        )

    my_cols = pl.ds(pl.multiple_of(me_t * Cl, Cl), Cl)
    mate_cols = pl.ds(pl.multiple_of((1 - me_t) * Cl, Cl), Cl)
    loads = [
        pltpu.make_async_copy(src, dst, lsem.at[n]) for n, (src, dst) in enumerate(((tw, twv), (sav, savv), (sw, swv)))
    ]
    mine = [
        pltpu.make_async_copy(og.at[pl.ds(f * Pl, Pl)], opad.at[pl.ds((f + 1) * Pl, Pl), my_cols], osem)
        for f in range(F)
    ]
    own_og = pltpu.make_async_copy(og, opad.at[pl.ds(Pl, F * Pl), my_cols], osem)
    for f in range(F):
        latl[f, pl.ds(WS, WS), :] = jnp.zeros((WS, Cl), BF16)
        latl[f, pl.ds((R + 2) * WS, WS), :] = jnp.zeros((WS, Cl), BF16)
    for copy in mine + loads:
        copy.start()

    with scope("barrier"):
        barrier = pltpu.get_barrier_semaphore()
        peers = [mate, near, (me_z, others[1], me_t), (me_z, others[2], me_t)]
        count = len(peers) + Z - 1
        for peer in peers:
            pl.semaphore_signal(barrier, inc=1, device_id=peer, device_id_type=MESH)
        for dz in range(1, Z):
            pl.semaphore_signal(
                barrier, inc=1, device_id=(lax.rem(me_z + dz, Z), me_s, me_t), device_id_type=MESH
            )
        pl.semaphore_wait(barrier, count)

    def frame(k):
        return jnp.where(me_u == 0, F - 1 - k, k)

    share = Cl // (2 * Z * U)

    def slice_of(u, c, z):
        return twx.at[:, pl.ds(pl.multiple_of(((u * 2 + c) * Z + z) * share, 16), share)]

    def slices(n):
        return twx.at[:, pl.ds(0, n * share)]

    here = pl.ds(pl.multiple_of(((me_u * 2 + me_c) * Z + me_z) * share, 16), share)
    x_mate = (me_z, others[1], me_t)
    wy = remote(tw.at[:, here], twx.at[:, here], wysem.at[0], wysem.at[1], mate)
    wy.start()
    ocopies = []
    for k in range(F):
        f = frame(k)
        copy = remote(og.at[block(f)], opad.at[block(f, Pl), my_cols], osend, orecv.at[k], mate)
        copy.start()
        ocopies.append(copy)
    for n in (1, 2, 0):
        src, dst = window(others[n])
        remote(lat.at[src], latl.at[me_s, dst], lxsem.at[0], lxsem.at[1], (me_z, others[n], me_t)).start()
    src, dst = window(me_s)
    own = pltpu.make_async_copy(lat.at[src], latl.at[me_s, dst], lsem.at[3])
    own.start()

    opad[pl.ds(0, Pl), :] = jnp.zeros((Pl, C), BF16)
    opad[pl.ds((F + 1) * Pl, Pl), :] = jnp.zeros((Pl, C), BF16)
    hwide[pl.ds(0, 8), :] = jnp.zeros((8, C), F32)
    hwide[pl.ds(8 + HW, 8), :] = jnp.zeros((8, C), F32)
    for b in range(3):
        hs[b, pl.ds(0, WS), :] = jnp.zeros((WS, C), BF16)
        hs[b, pl.ds(WS + HW, WS), :] = jnp.zeros((WS, C), BF16)
    with scope("load"):
        own_og.wait()
        for copy in loads:
            copy.wait()
    savt[...] = savv[...].T

    def pass_x(n):
        piece = slice_of(me_u, me_c, lax.rem(me_z + Z - n, Z))
        remote(piece, piece, wxsend, wxrecv.at[n], x_mate).start()
        remote(piece, piece, wcsem.at[0], wcsem.at[1], near).start()

    def pass_z(n):
        piece = slice_of(me_u, me_c, lax.rem(me_z + Z - n, Z))
        remote(piece, piece, wzsend, wzrecv.at[n - 1], (lax.rem(me_z + n, Z), me_s, me_t)).wait_recv()
        pass_x(n)

    def pass_core(n):
        piece = slice_of(1 - me_u, me_c, lax.rem(me_z + Z - n, Z))
        remote(piece, piece, wxsend, wxrecv.at[n], x_mate).wait_recv()
        remote(piece, piece, wcsem.at[0], wcsem.at[1], near).start()

    with scope("wy"):
        wy.wait()
    for dz in (1, Z - 1, 2):
        piece = slice_of(me_u, me_c, me_z)
        remote(piece, piece, wzsend, wzrecv.at[dz - 1], (lax.rem(me_z + dz, Z), me_s, me_t)).start()
    pass_x(0)

    with scope("passz"):
        pass_z(1)
        pass_z(Z - 1)
    with scope("lwait"):
        own.wait()
        part = lat.at[pl.ds(0, len(others) * (R + 2) * WS)]
        remote(part, part, lxsem.at[0], lxsem.at[1], near).wait()

    span = (R + 2) * WS
    column = lax.rem(lax.broadcasted_iota(jnp.int32, (span, Cl), 0), WS)

    def latents_of(f):
        lwide[...] = latl[f].astype(F32)
        for b in range(3):
            if b == 1:
                value = latl[f, pl.ds(WS, span), :]
            else:
                value = lwide[pl.ds(WS + b - 1, span), :]
                value = jnp.where(column != (WS - 1 if b == 2 else 0), value, 0.0).astype(BF16)
            for row in range(3):
                latt[3 * row + b, :, pl.ds(f * Pl, Pl)] = value[row * WS : row * WS + Pl].T

    def landing(n):
        return hs.at[1, block(n, WS), my_cols]

    def hidden(weights, at, size):
        total = None
        for k in range(KT):
            term = nt(opad[pl.ds(pl.multiple_of(at + (KT - 1 - k) * Pl, 16), size), :], weights[k])
            total = term if total is None else total + term
        return total.astype(BF16)

    arrived = 0

    def take(n):
        nonlocal arrived
        with scope(f"owait{n}"):
            while arrived < n:
                ocopies[arrived].wait_recv()
                arrived += 1

    for k in range(F - U):
        f = frame(k)
        with scope(f"lshift{k}"):
            for part_f in range(k * U, (k + 1) * U):
                latents_of(part_f)
        if k == 0:
            with scope("passz2"):
                pass_z(2)
        take(k + 2)
        with scope(f"hidden{k}"):
            hid[block(f), my_cols] = hidden(twv, f * Pl, Pl)
        copy = remote(
            hid.at[block(f), my_cols], landing(me_s), xsend, xrecv.at[lax.rem(f + me_c, 2)], (me_z, f, me_t)
        )
        copy.start()
        with scope(f"pass{k}"):
            for n in ((0, 1), (Z - 1, 2))[k]:
                pass_core(n)
    take(F)

    sent = {}

    def view(n):
        tap, at, rows = chunks[n]
        return tap, pl.ds(at, rows)

    def start1(n):
        at = view(n)
        sent[1, n] = remote(gsend.at[(1 - me_c, slice(None)) + at], g1.at[(slice(None),) + at], s1s, s1r.at[n], near)
        sent[1, n].start()

    def step1(n):
        at = view(n)
        sent[1, n].wait_recv()
        other = 1 - me_u
        g2s[at] = (gsend[(me_c, other) + at].astype(F32) + g1[(other,) + at].astype(F32)).astype(BF16)
        sent[2, n] = remote(g2s.at[at], g2r.at[at], s2s, s2r.at[n], (me_z, others[1], me_t))
        sent[2, n].start()

    half = Z // 2
    low = me_z < half
    is_end = jnp.logical_or(me_z == 0, me_z == Z - 1)
    is_inner = jnp.logical_or(me_z == half - 1, me_z == half)
    z_in = jnp.where(low, me_z + 1, me_z - 1)
    z_out = jnp.clip(jnp.where(low, me_z - 1, me_z + 1), 0, Z - 1)
    Z_INNER, Z_OUTER = 0, 1

    def hop(n, src, send, slot, target):
        at = view(n)
        return remote(src.at[at], gzr.at[(slot,) + at], s3s.at[send], s3r.at[slot, n], (target, me_s, me_t))

    def to_inner(n):
        return hop(n, gz, 0, Z_OUTER, z_in)

    def across(n):
        return hop(n, gz, 0, Z_INNER, z_in)

    def to_outer(n):
        return hop(n, gf, 1, Z_INNER, z_out)

    def result(n, value):
        at = view(n)
        sums[at] = value.astype(F32) * scale
        pltpu.make_async_copy(sums.at[at], sums_out.at[at], rsem).start()

    def step2(n):
        at = view(n)
        sent[2, n].wait_recv()
        total = gsend[(me_c, me_u) + at].astype(F32) + g1[(me_u,) + at].astype(F32)
        total = total + g2r[at].astype(F32)
        gzf[at] = total

        @pl.when(is_end)
        def _():
            gz[at] = total.astype(BF16)
            to_inner(n).start()

    def step3(n):
        at = view(n)

        @pl.when(is_inner)
        def _():
            to_inner(n).wait_recv()
            gz[at] = (gzf[at] + gzr[(Z_OUTER,) + at].astype(F32)).astype(BF16)
            across(n).start()

    def step4(n):
        at = view(n)

        @pl.when(is_inner)
        def _():
            across(n).wait_recv()
            value = (gz[at].astype(F32) + gzr[(Z_INNER,) + at].astype(F32)).astype(BF16)
            gf[at] = value
            to_outer(n).start()
            result(n, value)

    def step5(n):
        at = view(n)

        @pl.when(is_end)
        def _():
            across(n).wait_recv()
            result(n, gzr[(Z_INNER,) + at])

    def finish():
        remote(og, opad.at[pl.ds(Pl, F * Pl), my_cols], osend, orecv.at[0], mate).wait_send()
        part = hid.at[pl.ds(0, (F - U) * Pl), my_cols]
        remote(part, part, xsend, xrecv.at[0], x_mate).wait_send()
        remote(slices(Z - 1), slices(Z - 1), wzsend, wzrecv.at[0], (z_in, me_s, me_t)).wait_send()
        remote(slices(Z), slices(Z), wxsend, wxrecv.at[0], x_mate).wait_send()
        remote(gsend.at[1 - me_c], g1, s1s, s1r.at[0], near).wait_send()
        remote(g2s, g2r, s2s, s2r.at[0], (me_z, others[1], me_t)).wait_send()
        remote(gz, gzr.at[Z_INNER], s3s.at[0], s3r.at[0, 0], (z_in, me_s, me_t)).wait_send()

        @pl.when(is_inner)
        def _():
            remote(gf, gzr.at[Z_INNER], s3s.at[1], s3r.at[0, 0], (z_out, me_s, me_t)).wait_send()

        pltpu.make_async_copy(sums, sums_out, rsem).wait()

    def gradient(tap):
        if tap < KT:
            part = nn(savt[...], opad[pl.ds((KT - 1 - tap) * Pl, F * Pl), :])
        else:
            part = nn(latt[tap - KT], hid[...])
        for s in range(S):
            gsend[s % 2, s // 2, tap] = part[:, s * Cs : (s + 1) * Cs].astype(BF16)
        for n, chunk in enumerate(chunks):
            if chunk[0] == tap:
                start1(n)

    early = [n for n, chunk in enumerate(chunks) if chunk[0] < KT]
    for tap in range(KT):
        with scope(f"g_{tap}"):
            gradient(tap)
    with scope("early0"):
        for n in early[:2]:
            step1(n)
    with scope("hiddenown"):
        for k in range(F - U, F):
            f = frame(k)
            hid[block(f), my_cols] = hidden(twv, f * Pl, Pl)
    with scope("early"):
        for n in early[2:]:
            step1(n)
    with scope("wwait"):
        remote(slices(2 * Z), slices(2 * Z), wcsem.at[0], wcsem.at[1], near).wait()
    with scope("hiddenrest"):
        hid[:, mate_cols] = hidden(twx, 0, F * Pl)
    to_sib = remote(hid.at[block(sib)], hs.at[1, block(me_s, WS)], bsem.at[0], bsem.at[1], near)
    to_sib.start()
    with scope("relay"):
        for slot in range(2):
            source = others[1 + slot]
            remote(
                landing(source), landing(source), xsend, xrecv.at[slot], (me_z, source, me_t)
            ).wait_recv()
            remote(landing(source), landing(source), ysem.at[0], ysem.at[1], mate).start()

    def arrive():
        to_sib.wait()
        part = hs.at[1, pl.ds(pl.multiple_of(WS + far * Pl, 16), 2 * Pl), my_cols]
        remote(part, part, ysem.at[0], ysem.at[1], mate).wait()
        hs[1, block(me_s, WS), :] = hid[block(me_s), :]

    tile = 4 * WS

    def shift():
        for r in range(0, HW, tile):
            hwide[pl.ds(8 + r, tile), :] = hs[1, pl.ds(WS + r, tile), :].astype(F32)
        column = lax.rem(lax.broadcasted_iota(jnp.int32, (tile, C), 0), WS)
        for b in (-1, 1):
            keep = column != (0 if b == 1 else WS - 1)
            for r in range(0, HW, tile):
                value = hwide[pl.ds(8 + r - b, tile), :]
                hs[b + 1, pl.ds(WS + r, tile), :] = jnp.where(keep, value, 0.0).astype(BF16)

    images = 2 * swv.shape[0]
    image_out = pltpu.make_async_copy(ig, ig_out, isem)

    def image(n):
        tap, at = n // 2, (n % 2) * (HW // 2)
        row, col = tap // 3, tap % 3
        rows = pl.ds(at, HW // 2)
        term = nt(hs[col, pl.ds((2 - row) * WS + at, HW // 2), :], swv[tap])
        if tap == 0:
            acc[rows, :] = term
        elif n < images - 2:
            acc[rows, :] += term
        else:
            ig[rows, :] = (acc[rows, :] + term).astype(BF16)
        if n == images - 1:
            image_out.start()

    steps = {1: step1, 2: step2, 3: step3, 4: step4, 5: step5, "g": gradient, "i": image}
    for kind, n in order(chunks, KT, images, Cl):
        with scope(f"{kind}_{n}"):
            if kind == "h":
                arrive()
            elif kind == "s":
                shift()
            else:
                steps[kind](n)
    with scope("fin"):
        finish()
        image_out.wait()


def fused(sizes, latents, saved_input, out_grad, temporal_weight, spatial_weight):
    S, T, Z = sizes
    F, Pl, Cl = out_grad.shape[1:]
    KT, _, C = temporal_weight.shape
    taps = KT + spatial_weight.shape[0]
    HW = latents.shape[2]
    Cs = C // S
    U = S // 2
    scale = 1.0 / math.sqrt(Z * F * HS * WS)
    chunks = pieces_of(list(range(KT)) + [KT + tap for tap in FIRST], PARTS, Cl)
    N = len(chunks)
    dims = (S, T, Z, F, Pl, Cl, Cs, scale, chunks, KT)
    V = pltpu.VMEM
    D = pltpu.SemaphoreType.DMA
    hbm = pl.BlockSpec(memory_space=pltpu.HBM)
    vmem = pl.BlockSpec(memory_space=pltpu.VMEM)
    ig, sums = pl.pallas_call(
        functools.partial(kernel, dims),
        out_shape=(
            jax.ShapeDtypeStruct((HW, Cl), BF16),
            jax.ShapeDtypeStruct((taps, Cl, Cs), F32),
        ),
        in_specs=[hbm] * 5,
        out_specs=(pl.BlockSpec(memory_space=pl.ANY),) * 2,
        scratch_shapes=[
            V((F * Pl, Cl), BF16), V((KT, Cl, C), BF16), V((KT, Cl, C), BF16), V((taps - KT, Cl, C), BF16),
            V(((F + 2) * Pl, C), BF16), V((F * Pl, C), BF16), V((Cl, F * Pl), BF16),
            V((F, Pl + 4 * WS, Cl), BF16), V((Pl + 4 * WS, Cl), F32), V((taps - KT, Cl, F * Pl), BF16),
            V((HW + 16, C), F32), V((3, HW + 2 * WS, C), BF16), V((HW, Cl), F32),
            V((HW, Cl), BF16), V((taps, Cl, Cs), BF16), V((taps, Cl, Cs), F32),
            V((2, U, taps, Cl, Cs), BF16), V((U, taps, Cl, Cs), BF16), V((taps, Cl, Cs), BF16),
            V((taps, Cl, Cs), BF16), V((taps, Cl, Cs), BF16), V((taps, Cl, Cs), F32), V((2, taps, Cl, Cs), BF16),
            D((4,)), D(()), D((F,)), D(()), D(()), D((2,)), D((2,)), D((2,)), D((2,)),
            D((2,)), D(()), D((Z - 1,)), D(()), D((Z,)), D((2,)),
            D(()), D((N,)), D(()), D((N,)), D((2,)), D((2, N)), D(()), D(()),
        ],
        compiler_params=pltpu.CompilerParams(
            collective_id=0, has_side_effects=True, vmem_limit_bytes=40 * 2**20
        ),
    )(*(
        pltpu.with_memory_space_constraint(value, pltpu.HBM)
        for value in (
            latents.reshape(HW, Cl), saved_input.reshape(F * Pl, Cl), out_grad.reshape(F * Pl, Cl),
            temporal_weight, spatial_weight,
        )
    ))

    def finish(ig_ref, sums_ref, ig_out, tg_out, sg_out, sem):
        half = (taps - KT) // 2
        pairs = (
            (sums_ref.at[pl.ds(KT, half)], sg_out.at[pl.ds(0, half)]),
            (sums_ref.at[pl.ds(KT + half, taps - KT - half)], sg_out.at[pl.ds(half, taps - KT - half)]),
            (sums_ref.at[pl.ds(0, KT)], tg_out),
            (ig_ref, ig_out),
        )
        copies = [pltpu.make_async_copy(src, dst, sem.at[n]) for n, (src, dst) in enumerate(pairs)]
        for copy in copies:
            copy.start()
        for copy in copies:
            copy.wait()

    ig, tg, sg = pl.pallas_call(
        finish,
        out_shape=(
            jax.ShapeDtypeStruct((HW, Cl), BF16),
            jax.ShapeDtypeStruct((KT, Cl, Cs), F32),
            jax.ShapeDtypeStruct((taps - KT, Cl, Cs), F32),
        ),
        in_specs=[vmem] * 2,
        out_specs=(hbm,) * 3,
        scratch_shapes=[D((4,))],
        compiler_params=pltpu.CompilerParams(vmem_limit_bytes=16 * 2**20),
    )(ig, sums)
    return ig.reshape(latents.shape), tg, sg


def plain(latents, saved_input, out_grad, temporal_weight, spatial_weight):
    clips_all = latents.shape[0] * lax.axis_size("clip")
    frames_all = latents.shape[1] * lax.axis_size("sp")
    scale_factor = 1.0 / math.sqrt(clips_all * frames_all * HS * WS)
    frames_count = out_grad.shape[1]
    local_in = temporal_weight.shape[1]
    saved_padded = pad_frames(saved_input)
    block_in = lax.all_gather(out_grad, "tp", axis=3, tiled=True)
    padded = pad_frames(block_in)
    hidden_acc = jnp.zeros(out_grad.shape[:3] + (local_in,), F32)
    parts = []
    for tap_index in range(3):
        shifted = padded[:, 2 - tap_index : 2 - tap_index + frames_count]
        hidden_acc = hidden_acc + jnp.einsum(
            "bfpo,io->bfpi", shifted, temporal_weight[tap_index], preferred_element_type=F32
        )
        window = saved_padded[:, tap_index : tap_index + frames_count]
        parts.append(jnp.einsum("bfpi,bfpo->io", window, block_in, preferred_element_type=F32))
    temporal_local = jnp.stack(parts)
    hidden_grad = hidden_acc.astype(BF16)
    regrouped = lax.all_to_all(hidden_grad, "sp", split_axis=1, concat_axis=2, tiled=True)
    batch = latents.shape[0] * latents.shape[1]
    image_pad = jnp.pad(latents.reshape(batch, HS, WS, local_in), ((0, 0), (1, 1), (1, 1), (0, 0)))
    block_in = lax.all_gather(regrouped, "tp", axis=3, tiled=True)
    whole = block_in.reshape(batch, HS, WS, block_in.shape[3])
    grid = jnp.pad(whole, ((0, 0), (1, 1), (1, 1), (0, 0)))
    input_acc = jnp.zeros((batch, HS, WS, local_in), F32)
    parts = []
    for row in (-1, 0, 1):
        for col in (-1, 0, 1):
            tap_index = 3 * (row + 1) + (col + 1)
            moved = grid[:, 1 - row : 1 - row + HS, 1 - col : 1 - col + WS]
            input_acc = input_acc + jnp.einsum(
                "gabo,co->gabc", moved, spatial_weight[tap_index], preferred_element_type=F32
            )
            window = image_pad[:, 1 + row : 1 + row + HS, 1 + col : 1 + col + WS]
            parts.append(jnp.einsum("gabc,gabo->co", window, whole, preferred_element_type=F32))
    spatial_local = jnp.stack(parts)
    input_grad = input_acc.reshape(latents.shape).astype(BF16)
    temporal_grad, spatial_grad = lax.psum(
        tuple(
            lax.psum_scatter(value * scale_factor, "sp", scatter_dimension=2, tiled=True)
            for value in (temporal_local, spatial_local)
        ),
        "clip",
    )
    return input_grad, temporal_grad, spatial_grad


PARTS = [2, 1, 1, 1, 1, 1, 1, 1, 1, 1, 2, 4]
HOP = 2.1
START = -2.4
FIRST = [4, 3, 5, 0, 1, 2, 6, 7, 8]


def solution(mesh):
    sizes = (mesh.shape["sp"], mesh.shape["tp"], mesh.shape["clip"])

    def local(latents, saved_input, out_grad, temporal_weight, spatial_weight):
        S, T, Z = sizes
        cols = temporal_weight.shape[2] // S
        fits = (
            latents.shape[:2] == (1, 1) and S == out_grad.shape[1] == 4 and T == 2 and Z == 4
            and cols % 128 == 0 and out_grad.shape[3] % 256 == 0 and out_grad.shape[2] % 128 == 0
            and latents.shape[2] == HS * WS == S * out_grad.shape[2]
        )
        args = (latents, saved_input, out_grad, temporal_weight, spatial_weight)
        return fused(sizes, *args) if fits else plain(*args)

    return jax.shard_map(
        local,
        mesh=mesh,
        in_specs=(
            P("clip", "sp", None, "tp"),
            P("clip", None, "sp", "tp"),
            P("clip", None, "sp", "tp"),
            P(None, "tp", None),
            P(None, "tp", None),
        ),
        out_specs=(P("clip", "sp", None, "tp"), P(None, "tp", "sp"), P(None, "tp", "sp")),
        check_vma=False,
    )
```

```python
import contextlib
import functools
import math

import jax
import jax.numpy as jnp
from jax import lax
from jax.experimental import pallas as pl
from jax.experimental.pallas import tpu as pltpu
from jax.sharding import PartitionSpec as P

HS = 32
WS = 32
MESH = pl.DeviceIdType.MESH
F32 = jnp.float32
BF16 = jnp.bfloat16


def pad_frames(values):
    return jnp.pad(values, ((0, 0), (1, 1), (0, 0), (0, 0)))


def nt(a, b):
    return lax.dot_general(a, b, (((1,), (1,)), ((), ())), preferred_element_type=F32)


def nn(a, b):
    return lax.dot_general(a, b, (((1,), (0,)), ((), ())), preferred_element_type=F32)


scope = contextlib.nullcontext


def pieces_of(taps, parts, rows):
    return [(tap, part * (rows // n), rows // n) for tap, n in zip(taps, parts) for part in range(n)]


def order(chunks, lead, early_taps, images, rows):
    hop, core_hop, link, core = HOP, 0.65, 1.39, 0.44
    now, free = START, {"core": 0.0, "x": START, "z": LEAD, "across": 0.0, "back": 0.0}
    pending, out = {}, []

    def send(name, part, key, step=None):
        free[name] = max(free[name], now) + (core if name == "core" else link) * part
        pending[key] = free[name] + (core_hop if name == "core" else hop) + LATE.get(key[0], 0.0)

    taps = list(dict.fromkeys(tap for tap, _, _ in chunks))
    late = taps[early_taps:]
    filler = ["a"] + list(range(images // 2)) + ["h"] + list(range(images // 2, images))
    for n, chunk in enumerate(chunks):
        if chunk[0] not in late:
            send("x", chunk[2] / rows, (2, n))
    now = LEAD
    for n in range(lead):
        send("z", 2 / lead, ("B", n))
    now = 0.0
    gate = {"a": NEAR, "h": 1e9}
    pending["r", 0], pending["r", 1] = EARLY, EARLY + 1.4
    while pending or late or filler:
        ready = sorted((at, str(key), key) for key, at in pending.items() if at <= now)
        if ready:
            at, _, (step, n) = ready[0]
            del pending[step, n]
            out.append((step, n))
            if step == "r":
                now += 0.05
                gate["h"] = now + 2.5 * link + hop if n else gate["h"]
            elif isinstance(step, str):
                now += 0.05
                if step == "B":
                    send("across", 2 / lead, ("C", n))
                elif step == "C":
                    send("back", 2 / lead, ("D", n))
                elif step == "D":
                    send("x", 1 / lead, ("E", n))
            else:
                part = chunks[n][2] / rows
                now += 0.06 * part
                if step < 5:
                    send(("core", "x", "z", "across", "back")[step], part, (step + 1, n))
            continue
        soon = min(pending.values()) if pending else 1e9
        if late:
            tap = late.pop(0)
            out.append(("g", tap))
            now += 0.7 if len(taps) - early_taps - len(late) <= 3 else 0.45
            for n, chunk in enumerate(chunks):
                if chunk[0] == tap:
                    send("core", chunk[2] / rows, (1, n))
            continue
        at = gate.get(filler[0], 0.0) if filler else 0.0
        waits = now < at
        if filler and not waits and (soon > now + SLACK or not pending):
            kind = filler.pop(0)
            out.append((kind, 0) if isinstance(kind, str) else ("i", kind))
            now += 0.3
        else:
            now = max(now, min(soon, at) if waits else soon)
    return out


def kernel(
    dims, lat, sav, og, tw, sw, ig_out, sums_out,
    savv, twv, twx, swv, opad, hid, savt, most, latl, lwide, latt, hs, acc, ig, gf, sums,
    gsend, g1, g2s, g2r, gz, gzf, gzr, qs, qf, qr, qown, qx,
    lsem, osend, orecv, osem, xsend, xrecv, bsem, ysem, lxsem, wysem, wzsend, wzrecv, wxsend, wxrecv, wcsem,
    s1s, s1r, s2s, s2r, s3s, s3r, isem, rsem, entered, qcore, qsem, qrecv, qxrecv,
):
    S, T, Z, F, Pl, Cl, Cs, scale, chunks, KT = dims
    U = S // 2
    HW = S * Pl
    C = T * Cl
    R = Pl // WS
    me_s, me_t, me_z = lax.axis_index("sp"), lax.axis_index("tp"), lax.axis_index("clip")
    me_u, me_c = me_s // 2, lax.rem(me_s, 2)
    sib = me_u * 2 + 1 - me_c
    far = (1 - me_u) * 2
    mate = (me_z, me_s, 1 - me_t)
    near = (me_z, sib, me_t)
    others = (sib, far + me_c, far + 1 - me_c)

    def remote(src, dst, send, recv, device):
        return pltpu.make_async_remote_copy(
            src_ref=src, dst_ref=dst, send_sem=send, recv_sem=recv, device_id=device, device_id_type=MESH
        )

    def block(n, base=0):
        return pl.ds(pl.multiple_of(base + n * Pl, 16), Pl)

    def window(n):
        at = jnp.clip(n * R - 1, 0, HW // WS - R - 2)
        return (
            pl.ds(pl.multiple_of(at * WS, WS), (R + 2) * WS),
            pl.ds(pl.multiple_of((at - n * R + 2) * WS, WS), (R + 2) * WS),
        )

    my_cols = pl.ds(pl.multiple_of(me_t * Cl, Cl), Cl)
    mate_cols = pl.ds(pl.multiple_of((1 - me_t) * Cl, Cl), Cl)
    loads = [
        pltpu.make_async_copy(src, dst, lsem.at[n]) for n, (src, dst) in enumerate(((tw, twv), (sav, savv), (sw, swv)))
    ]
    mine = [
        pltpu.make_async_copy(og.at[pl.ds(f * Pl, Pl)], opad.at[pl.ds((f + 1) * Pl, Pl), my_cols], osem)
        for f in range(F)
    ]
    own_og = pltpu.make_async_copy(og, opad.at[pl.ds(Pl, F * Pl), my_cols], osem)
    for f in range(F):
        latl[f, pl.ds(WS, WS), :] = jnp.zeros((WS, Cl), BF16)
        latl[f, pl.ds((R + 2) * WS, WS), :] = jnp.zeros((WS, Cl), BF16)
    for copy in mine + loads:
        copy.start()

    with scope("barrier"):
        barrier = pltpu.get_barrier_semaphore()
        peers = [mate, near, (me_z, others[1], me_t), (me_z, others[2], me_t)]
        first, last = me_z == 0, me_z == Z - 1
        count = len(peers) + jnp.where(jnp.logical_or(first, last), 1, 2)
        for peer in peers:
            pl.semaphore_signal(barrier, inc=1, device_id=peer, device_id_type=MESH)

        def tell(semaphore, step, sends):
            @pl.when(sends)
            def _():
                pl.semaphore_signal(
                    semaphore, inc=1, device_id=(jnp.clip(me_z + step, 0, Z - 1), me_s, me_t), device_id_type=MESH
                )

        tell(barrier, 1, jnp.logical_not(last))
        tell(barrier, -1, jnp.logical_not(first))
        pl.semaphore_wait(barrier, count)
        tell(entered.at[0], 1, me_z == 1)
        tell(entered.at[1], -1, me_z == Z - 2)

    def frame(k):
        return jnp.where(me_u == 0, F - 1 - k, k)

    share = Cl // (2 * Z * U)

    def slice_of(u, c, z):
        return twx.at[:, pl.ds(pl.multiple_of(((u * 2 + c) * Z + z) * share, 16), share)]

    def slices(n):
        return twx.at[:, pl.ds(0, n * share)]

    here = pl.ds(pl.multiple_of(((me_u * 2 + me_c) * Z + me_z) * share, 16), share)
    x_mate = (me_z, others[1], me_t)
    wy = remote(tw.at[:, here], twx.at[:, here], wysem.at[0], wysem.at[1], mate)
    wy.start()
    ocopies = []
    for k in range(F):
        f = frame(k)
        copy = remote(og.at[block(f)], opad.at[block(f, Pl), my_cols], osend, orecv.at[k], mate)
        copy.start()
        ocopies.append(copy)
    for n in (1, 2, 0):
        src, dst = window(others[n])
        remote(lat.at[src], latl.at[me_s, dst], lxsem.at[0], lxsem.at[1], (me_z, others[n], me_t)).start()
    src, dst = window(me_s)
    own = pltpu.make_async_copy(lat.at[src], latl.at[me_s, dst], lsem.at[3])
    own.start()

    opad[pl.ds(0, Pl), :] = jnp.zeros((Pl, C), BF16)
    opad[pl.ds((F + 1) * Pl, Pl), :] = jnp.zeros((Pl, C), BF16)
    for b in range(3):
        hs[b, pl.ds(0, WS), :] = jnp.zeros((WS, C), BF16)
        hs[b, pl.ds(WS + HW, WS), :] = jnp.zeros((WS, C), BF16)
    with scope("load"):
        own_og.wait()
        for copy in loads:
            copy.wait()
    savt[:, pl.ds(0, Pl)] = jnp.zeros((Cl, Pl), BF16)
    savt[:, pl.ds((F + 1) * Pl, Pl)] = jnp.zeros((Cl, Pl), BF16)
    savt[:, pl.ds(Pl, F * Pl)] = savv[...].T

    def pass_x(n):
        piece = slice_of(me_u, me_c, lax.rem(me_z + Z - n, Z))
        remote(piece, piece, wxsend, wxrecv.at[n], x_mate).start()
        remote(piece, piece, wcsem.at[0], wcsem.at[1], near).start()

    def pass_z(n):
        piece = slice_of(me_u, me_c, lax.rem(me_z + Z - n, Z))
        remote(piece, piece, wzsend, wzrecv.at[n - 1], (lax.rem(me_z + n, Z), me_s, me_t)).wait_recv()
        pass_x(n)

    def pass_core(n):
        piece = slice_of(1 - me_u, me_c, lax.rem(me_z + Z - n, Z))
        remote(piece, piece, wxsend, wxrecv.at[n], x_mate).wait_recv()
        remote(piece, piece, wcsem.at[0], wcsem.at[1], near).start()

    def hear(semaphore, step, hears, sends):
        @pl.when(hears)
        def _():
            pl.semaphore_wait(semaphore, 1)

        tell(semaphore, step, sends)

    with scope("wy"):
        wy.wait()
        hear(entered.at[0], 1, me_z >= 2, jnp.logical_and(me_z >= 2, me_z < Z - 1))
        hear(entered.at[1], -1, me_z <= Z - 3, jnp.logical_and(me_z <= Z - 3, me_z > 0))
    for dz in (1, Z - 1, 2):
        piece = slice_of(me_u, me_c, me_z)
        remote(piece, piece, wzsend, wzrecv.at[dz - 1], (lax.rem(me_z + dz, Z), me_s, me_t)).start()
    pass_x(0)

    with scope("passz"):
        pass_z(1)
        pass_z(Z - 1)
    with scope("lwait"):
        own.wait()
        part = lat.at[pl.ds(0, len(others) * (R + 2) * WS)]
        remote(part, part, lxsem.at[0], lxsem.at[1], near).wait()

    span = (R + 2) * WS
    column = lax.rem(lax.broadcasted_iota(jnp.int32, (span, Cl), 0), WS)

    def latents_of(f):
        lwide[...] = latl[f].astype(F32)
        for b in range(3):
            if b == 1:
                value = latl[f, pl.ds(WS, span), :]
            else:
                value = lwide[pl.ds(WS + b - 1, span), :]
                value = jnp.where(column != (WS - 1 if b == 2 else 0), value, 0.0).astype(BF16)
            for row in range(3):
                latt[3 * row + b, :, pl.ds(f * Pl, Pl)] = value[row * WS : row * WS + Pl].T

    def landing(n, part):
        at = pl.multiple_of(WS + n * Pl + part * (Pl // 2), 16)
        return hs.at[1, pl.ds(at, Pl // 2), my_cols]

    def send_block(k, parts=(0, 1)):
        f = frame(k)
        for part in parts:
            rows = pl.ds(pl.multiple_of(f * Pl + part * (Pl // 2), 16), Pl // 2)
            remote(
                hid.at[rows, my_cols], landing(me_s, part),
                xsend, xrecv.at[part, lax.rem(f + me_c, 2)], (me_z, f, me_t),
            ).start()

    def hidden(weights, at, size):
        total = None
        for k in range(KT):
            term = nt(opad[pl.ds(pl.multiple_of(at + (KT - 1 - k) * Pl, 16), size), :], weights[k])
            total = term if total is None else total + term
        return total.astype(BF16)

    arrived = 0

    def take(n):
        nonlocal arrived
        with scope(f"owait{n}"):
            while arrived < n:
                ocopies[arrived].wait_recv()
                arrived += 1

    for k in range(F - U):
        f = frame(k)
        if k == 0:
            with scope("lshift0"):
                for part_f in range(U):
                    latents_of(part_f)
            with scope("passz2"):
                pass_z(2)
        take(k + 2)
        with scope(f"hidden{k}"):
            hid[block(f), my_cols] = hidden(twv, f * Pl, Pl)
        send_block(k)
        if k == 0:
            with scope("lshift1"):
                for part_f in range(U, F):
                    latents_of(part_f)
    with scope("passc"):
        pass_core(0)
        pass_core(1)
    base = jnp.where(me_u == 0, U, 1)
    for tap in range(KT):
        with scope(f"p_{tap}"):
            at = pl.multiple_of((base + tap - 1) * Pl, 128)
            most[tap] = nn(
                savt[:, pl.ds(at, (F - 1) * Pl)], opad[pl.ds(pl.multiple_of(base * Pl, 16), (F - 1) * Pl), :]
            )
    take(F)

    sent = {}

    def view(n):
        tap, at, rows = chunks[n]
        return tap, pl.ds(at, rows)

    def start1(n):
        at = view(n)
        sent[1, n] = remote(gsend.at[(1 - me_c, slice(None)) + at], g1.at[(slice(None),) + at], s1s, s1r.at[n], near)
        sent[1, n].start()

    def step1(n):
        at = view(n)
        sent[1, n].wait_recv()
        other = 1 - me_u
        g2s[at] = (gsend[(me_c, other) + at].astype(F32) + g1[(other,) + at].astype(F32)).astype(BF16)
        sent[2, n] = remote(g2s.at[at], g2r.at[at], s2s, s2r.at[n], (me_z, others[1], me_t))
        sent[2, n].start()

    half = Z // 2
    low = me_z < half
    is_end = jnp.logical_or(me_z == 0, me_z == Z - 1)
    is_inner = jnp.logical_or(me_z == half - 1, me_z == half)
    z_in = jnp.where(low, me_z + 1, me_z - 1)
    z_out = jnp.clip(jnp.where(low, me_z - 1, me_z + 1), 0, Z - 1)
    Z_INNER, Z_OUTER = 0, 1

    def hop(n, src, send, slot, target):
        at = view(n)
        return remote(src.at[at], gzr.at[(slot,) + at], s3s.at[send], s3r.at[slot, n], (target, me_s, me_t))

    def to_inner(n):
        return hop(n, gz, 0, Z_OUTER, z_in)

    def across(n):
        return hop(n, gz, 0, Z_INNER, z_in)

    def to_outer(n):
        return hop(n, gf, 1, Z_INNER, z_out)

    def result(n, value):
        at = view(n)
        sums[at] = value.astype(F32) * scale
        pltpu.make_async_copy(sums.at[at], sums_out.at[at], rsem).start()

    def step2(n):
        at = view(n)
        sent[2, n].wait_recv()
        total = gsend[(me_c, me_u) + at].astype(F32) + g1[(me_u,) + at].astype(F32)
        total = total + g2r[at].astype(F32)
        gzf[at] = total

        @pl.when(is_end)
        def _():
            gz[at] = total.astype(BF16)
            to_inner(n).start()

    def step3(n):
        at = view(n)

        @pl.when(is_inner)
        def _():
            to_inner(n).wait_recv()
            gz[at] = (gzf[at] + gzr[(Z_OUTER,) + at].astype(F32)).astype(BF16)
            across(n).start()

    def step4(n):
        at = view(n)

        @pl.when(is_inner)
        def _():
            across(n).wait_recv()
            value = (gz[at].astype(F32) + gzr[(Z_INNER,) + at].astype(F32)).astype(BF16)
            gf[at] = value
            to_outer(n).start()
            result(n, value)

    def step5(n):
        at = view(n)

        @pl.when(is_end)
        def _():
            across(n).wait_recv()
            result(n, gzr[(Z_INNER,) + at])

    def finish():
        remote(og, opad.at[pl.ds(Pl, F * Pl), my_cols], osend, orecv.at[0], mate).wait_send()
        part = hid.at[pl.ds(0, (F - U) * Pl), my_cols]
        remote(part, part, xsend, xrecv.at[0, 0], x_mate).wait_send()
        remote(slices(Z - 1), slices(Z - 1), wzsend, wzrecv.at[0], (z_in, me_s, me_t)).wait_send()
        remote(slices(Z), slices(Z), wxsend, wxrecv.at[0], x_mate).wait_send()
        remote(gsend.at[1 - me_c], g1, s1s, s1r.at[0], near).wait_send()
        remote(g2s, g2r, s2s, s2r.at[0], (me_z, others[1], me_t)).wait_send()
        rest = pl.ds(1, gz.shape[0] - 1)
        remote(gz.at[rest], gzr.at[Z_INNER, rest], s3s.at[0], s3r.at[0, 0], (z_in, me_s, me_t)).wait_send()
        remote(qs, qr.at[Z_INNER], qsem.at[0], qrecv.at[0, 0], (z_in, me_s, me_t)).wait_send()

        @pl.when(is_inner)
        def _():
            remote(gf.at[rest], gzr.at[Z_INNER, rest], s3s.at[1], s3r.at[0, 0], (z_out, me_s, me_t)).wait_send()
            remote(qf, qr.at[Z_INNER], qsem.at[1], qrecv.at[0, 0], (z_out, me_s, me_t)).wait_send()

        pltpu.make_async_copy(sums, sums_out, rsem).wait()

    def gradient(tap):
        if tap < KT:
            f = frame(F - 1)
            at = pl.multiple_of((f + tap) * Pl, 128)
            part = most[tap] + nn(savt[:, pl.ds(at, Pl)], opad[block(f, Pl), :])
        else:
            part = nn(latt[tap - KT], hid[...])
        for s in range(S):
            gsend[s % 2, s // 2, tap] = part[:, s * Cs : (s + 1) * Cs].astype(BF16)
        for n, chunk in enumerate(chunks):
            if chunk[0] == tap:
                start1(n)
        if tap == 0:
            for n in range(LEADS):
                rows = lead_rows(n)
                remote(gsend.at[1 - me_c, :, 0, rows], g1.at[:, 0, rows], s1s, qcore.at[n], near).start()

    piece_rows = Cl // LEADS

    def lead_rows(n):
        return pl.ds(n * piece_rows, piece_rows)

    def lead_hop(n, src, send, slot, target):
        return remote(
            src.at[:, lead_rows(n)], qr.at[slot, :, lead_rows(n)], qsem.at[send], qrecv.at[slot, n],
            (target, me_s, me_t),
        )

    def lead_a(n):
        rows = lead_rows(n)
        remote(gsend.at[1 - me_c, :, 0, rows], g1.at[:, 0, rows], s1s, qcore.at[n], near).wait_recv()
        total = gsend[me_c, :, 0, rows].astype(F32) + g1[:, 0, rows].astype(F32)

        @pl.when(is_end)
        def _():
            qs[:, rows] = total.astype(BF16)
            lead_hop(n, qs, 0, Z_OUTER, z_in).start()

        @pl.when(is_inner)
        def _():
            qown[:, rows] = total

    def lead_b(n):
        rows = lead_rows(n)

        @pl.when(is_inner)
        def _():
            lead_hop(n, qs, 0, Z_OUTER, z_in).wait_recv()
            qs[:, rows] = (qown[:, rows] + qr[Z_OUTER, :, rows].astype(F32)).astype(BF16)
            lead_hop(n, qs, 0, Z_INNER, z_in).start()

    def lead_x(n, src):
        return remote(src.at[lead_rows(n)], qx.at[lead_rows(n)], s2s, qxrecv.at[n], x_mate)

    def lead_c(n):
        rows = lead_rows(n)

        @pl.when(is_inner)
        def _():
            lead_hop(n, qs, 0, Z_INNER, z_in).wait_recv()
            qf[:, rows] = (qs[:, rows].astype(F32) + qr[Z_INNER, :, rows].astype(F32)).astype(BF16)
            lead_hop(n, qf, 1, Z_INNER, z_out).start()
            lead_x(n, qf.at[1 - me_u]).start()

    def lead_d(n):
        @pl.when(is_end)
        def _():
            lead_hop(n, qs, 0, Z_INNER, z_in).wait_recv()
            lead_x(n, qr.at[Z_INNER, 1 - me_u]).start()

    def lead_e(n):
        rows = lead_rows(n)
        lead_x(n, qf.at[1 - me_u]).wait_recv()

        def done(mine):
            sums[0, rows] = (mine.astype(F32) + qx[rows].astype(F32)) * scale
            pltpu.make_async_copy(sums.at[0, rows], sums_out.at[0, rows], rsem).start()

        @pl.when(is_inner)
        def _():
            done(qf[me_u, rows])

        @pl.when(is_end)
        def _():
            done(qr[Z_INNER, me_u, rows])

    early = [n for n, chunk in enumerate(chunks) if chunk[0] < KT]
    for tap in range(KT):
        with scope(f"g_{tap}"):
            gradient(tap)
        if tap == 0:
            with scope("passd"):
                pass_core(Z - 1)
                pass_core(2)
    with scope("early0"):
        for n in range(LEADS):
            lead_a(n)
    with scope("hiddenown"):
        for k in range(F - U, F):
            f = frame(k)
            hid[block(f), my_cols] = hidden(twv, f * Pl, Pl)
    with scope("early"):
        for n in early:
            step1(n)
    with scope("wwait"):
        remote(slices(2 * Z), slices(2 * Z), wcsem.at[0], wcsem.at[1], near).wait()
    with scope("hiddenrest"):
        hid[:, mate_cols] = hidden(twx, 0, F * Pl)
    to_sib = remote(hid.at[block(sib)], hs.at[1, block(me_s, WS)], bsem.at[0], bsem.at[1], near)
    to_sib.start()
    def relay(part):
        for slot in range(2):
            piece = landing(others[1 + slot], part)
            remote(piece, piece, xsend, xrecv.at[part, slot], (me_z, others[1 + slot], me_t)).wait_recv()
            remote(piece, piece, ysem.at[0], ysem.at[1], mate).start()

    def arrive_near():
        to_sib.wait()
        hs[1, block(me_s, WS), :] = hid[block(me_s), :]
        shift(me_u * (HW // 2))

    def arrive_far():
        part = hs.at[1, pl.ds(pl.multiple_of(WS + far * Pl, 16), 2 * Pl), my_cols]
        remote(part, part, ysem.at[0], ysem.at[1], mate).wait()
        shift((1 - me_u) * (HW // 2))

    tile = 4 * WS

    def shift(base):
        column = lax.rem(lax.broadcasted_iota(jnp.int32, (tile, C), 0), WS)
        for r in range(0, HW // 2, tile):
            rows = pl.ds(pl.multiple_of(base + WS + r, WS), tile)
            value = hs[1, rows, :].astype(F32)
            for b in (-1, 1):
                keep = column != (0 if b == 1 else WS - 1)
                moved = pltpu.roll(value, 1 if b == 1 else tile - 1, 0)
                hs[b + 1, rows, :] = jnp.where(keep, moved, 0.0).astype(BF16)

    images = 2 * swv.shape[0]
    image_out = pltpu.make_async_copy(ig, ig_out, isem)
    near_rows, far_rows = HW // 2 - WS, HW // 2 + WS
    near_at = me_u * far_rows
    far_at = (1 - me_u) * near_rows

    def image(n):
        tap = n % (images // 2)
        row, col = tap // 3, tap % 3
        at, size = (near_at, near_rows) if n < images // 2 else (far_at, far_rows)
        rows = pl.ds(pl.multiple_of(at, WS), size)
        term = nt(hs[col, pl.ds(pl.multiple_of(at + (2 - row) * WS, WS), size), :], swv[tap])
        if tap == 0:
            acc[rows, :] = term
        elif tap < images // 2 - 1:
            acc[rows, :] += term
        else:
            ig[rows, :] = (acc[rows, :] + term).astype(BF16)
        if n == images - 1:
            image_out.start()

    steps = {"B": lead_b, "C": lead_c, "D": lead_d, "E": lead_e}
    steps |= {1: step1, 2: step2, 3: step3, 4: step4, 5: step5, "g": gradient, "i": image}
    for kind, n in order(chunks, LEADS, KT - 1, images, Cl):
        with scope(f"{kind}_{n}"):
            if kind == "r":
                relay(n)
            elif kind == "a":
                arrive_near()
            elif kind == "h":
                arrive_far()
            else:
                steps[kind](n)
    with scope("fin"):
        finish()
        image_out.wait()


def fused(sizes, latents, saved_input, out_grad, temporal_weight, spatial_weight):
    S, T, Z = sizes
    F, Pl, Cl = out_grad.shape[1:]
    KT, _, C = temporal_weight.shape
    taps = KT + spatial_weight.shape[0]
    HW = latents.shape[2]
    Cs = C // S
    U = S // 2
    scale = 1.0 / math.sqrt(Z * F * HS * WS)
    chunks = pieces_of(list(range(1, KT)) + [KT + tap for tap in FIRST], PARTS, Cl)
    N = len(chunks)
    dims = (S, T, Z, F, Pl, Cl, Cs, scale, chunks, KT)
    V = pltpu.VMEM
    D = pltpu.SemaphoreType.DMA
    hbm = pl.BlockSpec(memory_space=pltpu.HBM)
    vmem = pl.BlockSpec(memory_space=pltpu.VMEM)
    ig, sums = pl.pallas_call(
        functools.partial(kernel, dims),
        out_shape=(
            jax.ShapeDtypeStruct((HW, Cl), BF16),
            jax.ShapeDtypeStruct((taps, Cl, Cs), F32),
        ),
        in_specs=[hbm] * 5,
        out_specs=(pl.BlockSpec(memory_space=pl.ANY),) * 2,
        scratch_shapes=[
            V((F * Pl, Cl), BF16), V((KT, Cl, C), BF16), V((KT, Cl, C), BF16), V((taps - KT, Cl, C), BF16),
            V(((F + 2) * Pl, C), BF16), V((F * Pl, C), BF16), V((Cl, (F + 2) * Pl), BF16), V((KT, Cl, C), F32),
            V((F, Pl + 4 * WS, Cl), BF16), V((Pl + 4 * WS, Cl), F32), V((taps - KT, Cl, F * Pl), BF16),
            V((3, HW + 2 * WS, C), BF16), V((HW, Cl), F32),
            V((HW, Cl), BF16), V((taps, Cl, Cs), BF16), V((taps, Cl, Cs), F32),
            V((2, U, taps, Cl, Cs), BF16), V((U, taps, Cl, Cs), BF16), V((taps, Cl, Cs), BF16),
            V((taps, Cl, Cs), BF16), V((taps, Cl, Cs), BF16), V((taps, Cl, Cs), F32), V((2, taps, Cl, Cs), BF16),
            V((U, Cl, Cs), BF16), V((U, Cl, Cs), BF16), V((2, U, Cl, Cs), BF16), V((U, Cl, Cs), F32), V((Cl, Cs), BF16),
            D((4,)), D(()), D((F,)), D(()), D(()), D((2, 2)), D((2,)), D((2,)), D((2,)),
            D((2,)), D(()), D((Z - 1,)), D(()), D((Z,)), D((2,)),
            D(()), D((N,)), D(()), D((N,)), D((2,)), D((2, N)), D(()), D(()), pltpu.SemaphoreType.REGULAR((2,)),
            D((LEADS,)), D((2,)), D((2, LEADS)), D((LEADS,)),
        ],
        compiler_params=pltpu.CompilerParams(
            collective_id=0, has_side_effects=True, vmem_limit_bytes=44 * 2**20
        ),
    )(*(
        pltpu.with_memory_space_constraint(value, pltpu.HBM)
        for value in (
            latents.reshape(HW, Cl), saved_input.reshape(F * Pl, Cl), out_grad.reshape(F * Pl, Cl),
            temporal_weight, spatial_weight,
        )
    ))

    def finish(ig_ref, sums_ref, ig_out, tg_out, sg_out, sem):
        half = (taps - KT) // 2
        pairs = (
            (sums_ref.at[pl.ds(KT, half)], sg_out.at[pl.ds(0, half)]),
            (sums_ref.at[pl.ds(KT + half, taps - KT - half)], sg_out.at[pl.ds(half, taps - KT - half)]),
            (sums_ref.at[pl.ds(0, KT)], tg_out),
            (ig_ref, ig_out),
        )
        copies = [pltpu.make_async_copy(src, dst, sem.at[n]) for n, (src, dst) in enumerate(pairs)]
        for copy in copies:
            copy.start()
        for copy in copies:
            copy.wait()

    ig, tg, sg = pl.pallas_call(
        finish,
        out_shape=(
            jax.ShapeDtypeStruct((HW, Cl), BF16),
            jax.ShapeDtypeStruct((KT, Cl, Cs), F32),
            jax.ShapeDtypeStruct((taps - KT, Cl, Cs), F32),
        ),
        in_specs=[vmem] * 2,
        out_specs=(hbm,) * 3,
        scratch_shapes=[D((4,))],
        compiler_params=pltpu.CompilerParams(vmem_limit_bytes=16 * 2**20),
    )(ig, sums)
    return ig.reshape(latents.shape), tg, sg


def plain(latents, saved_input, out_grad, temporal_weight, spatial_weight):
    clips_all = latents.shape[0] * lax.axis_size("clip")
    frames_all = latents.shape[1] * lax.axis_size("sp")
    scale_factor = 1.0 / math.sqrt(clips_all * frames_all * HS * WS)
    frames_count = out_grad.shape[1]
    local_in = temporal_weight.shape[1]
    saved_padded = pad_frames(saved_input)
    block_in = lax.all_gather(out_grad, "tp", axis=3, tiled=True)
    padded = pad_frames(block_in)
    hidden_acc = jnp.zeros(out_grad.shape[:3] + (local_in,), F32)
    parts = []
    for tap_index in range(3):
        shifted = padded[:, 2 - tap_index : 2 - tap_index + frames_count]
        hidden_acc = hidden_acc + jnp.einsum(
            "bfpo,io->bfpi", shifted, temporal_weight[tap_index], preferred_element_type=F32
        )
        window = saved_padded[:, tap_index : tap_index + frames_count]
        parts.append(jnp.einsum("bfpi,bfpo->io", window, block_in, preferred_element_type=F32))
    temporal_local = jnp.stack(parts)
    hidden_grad = hidden_acc.astype(BF16)
    regrouped = lax.all_to_all(hidden_grad, "sp", split_axis=1, concat_axis=2, tiled=True)
    batch = latents.shape[0] * latents.shape[1]
    image_pad = jnp.pad(latents.reshape(batch, HS, WS, local_in), ((0, 0), (1, 1), (1, 1), (0, 0)))
    block_in = lax.all_gather(regrouped, "tp", axis=3, tiled=True)
    whole = block_in.reshape(batch, HS, WS, block_in.shape[3])
    grid = jnp.pad(whole, ((0, 0), (1, 1), (1, 1), (0, 0)))
    input_acc = jnp.zeros((batch, HS, WS, local_in), F32)
    parts = []
    for row in (-1, 0, 1):
        for col in (-1, 0, 1):
            tap_index = 3 * (row + 1) + (col + 1)
            moved = grid[:, 1 - row : 1 - row + HS, 1 - col : 1 - col + WS]
            input_acc = input_acc + jnp.einsum(
                "gabo,co->gabc", moved, spatial_weight[tap_index], preferred_element_type=F32
            )
            window = image_pad[:, 1 + row : 1 + row + HS, 1 + col : 1 + col + WS]
            parts.append(jnp.einsum("gabc,gabo->co", window, whole, preferred_element_type=F32))
    spatial_local = jnp.stack(parts)
    input_grad = input_acc.reshape(latents.shape).astype(BF16)
    temporal_grad, spatial_grad = lax.psum(
        tuple(
            lax.psum_scatter(value * scale_factor, "sp", scatter_dimension=2, tiled=True)
            for value in (temporal_local, spatial_local)
        ),
        "clip",
    )
    return input_grad, temporal_grad, spatial_grad


PARTS = [4, 4, 2, 2, 2, 2, 2, 2, 2, 2, 4]
HOP = 2.1
START = -1.0
LEAD = -2.6
LEADS = 4
NEAR = 3.0
EARLY = 1.5
SLACK = 0.3
LATE = {5: 3.0, "E": 2.0}
FIRST = [4, 3, 5, 0, 1, 2, 6, 7, 8]


def solution(mesh):
    sizes = (mesh.shape["sp"], mesh.shape["tp"], mesh.shape["clip"])

    def local(latents, saved_input, out_grad, temporal_weight, spatial_weight):
        S, T, Z = sizes
        cols = temporal_weight.shape[2] // S
        fits = (
            latents.shape[:2] == (1, 1) and S == out_grad.shape[1] == 4 and T == 2 and Z == 4
            and cols % 128 == 0 and out_grad.shape[3] % 256 == 0 and out_grad.shape[2] % 128 == 0
            and latents.shape[2] == HS * WS == S * out_grad.shape[2]
        )
        args = (latents, saved_input, out_grad, temporal_weight, spatial_weight)
        return fused(sizes, *args) if fits else plain(*args)

    return jax.shard_map(
        local,
        mesh=mesh,
        in_specs=(
            P("clip", "sp", None, "tp"),
            P("clip", None, "sp", "tp"),
            P("clip", None, "sp", "tp"),
            P(None, "tp", None),
            P(None, "tp", None),
        ),
        out_specs=(P("clip", "sp", None, "tp"), P(None, "tp", "sp"), P(None, "tp", "sp")),
        check_vma=False,
    )
```

```python
import contextlib
import functools
import math

import jax
import jax.numpy as jnp
from jax import lax
from jax.experimental import pallas as pl
from jax.experimental.pallas import tpu as pltpu
from jax.sharding import PartitionSpec as P

HS = 32
WS = 32
MESH = pl.DeviceIdType.MESH
F32 = jnp.float32
BF16 = jnp.bfloat16


def pad_frames(values):
    return jnp.pad(values, ((0, 0), (1, 1), (0, 0), (0, 0)))


def nt(a, b):
    return lax.dot_general(a, b, (((1,), (1,)), ((), ())), preferred_element_type=F32)


def nn(a, b):
    return lax.dot_general(a, b, (((1,), (0,)), ((), ())), preferred_element_type=F32)


scope = contextlib.nullcontext


def pieces_of(taps, parts, rows):
    return [(tap, part * (rows // n), rows // n) for tap, n in zip(taps, parts) for part in range(n)]


def order(chunks, lead, early_taps, images, rows):
    hop, core_hop, link, core = HOP, 0.65, 1.39, 0.44
    now, free = START, {"core": 0.0, "x": START, "z": LEAD, "across": 0.0, "back": 0.0}
    pending, out = {}, []

    def send(name, part, key, step=None):
        free[name] = max(free[name], now) + (core if name == "core" else link) * part
        pending[key] = free[name] + (core_hop if name == "core" else hop) + LATE.get(key[0], 0.0)

    taps = list(dict.fromkeys(tap for tap, _, _ in chunks))
    late = taps[early_taps:]
    filler = ["a"] + list(range(images // 2)) + ["h"] + list(range(images // 2, images))
    for n, chunk in enumerate(chunks):
        if chunk[0] not in late:
            send("x", chunk[2] / rows, (2, n))
    now = LEAD
    for n in range(lead):
        send("z", 2 / lead, ("B", n))
    now = 0.0
    gate = {"a": NEAR, "h": 1e9}
    pending["r", 0], pending["r", 1] = EARLY, EARLY + 1.4
    while pending or late or filler:
        ready = sorted((at, str(key), key) for key, at in pending.items() if at <= now)
        if ready:
            at, _, (step, n) = ready[0]
            del pending[step, n]
            out.append((step, n))
            if step == "r":
                now += 0.05
                gate["h"] = now + 2.5 * link + hop if n else gate["h"]
            elif isinstance(step, str):
                now += 0.05
                if step == "B":
                    send("across", 2 / lead, ("C", n))
                elif step == "C":
                    send("back", 2 / lead, ("D", n))
                elif step == "D":
                    send("x", 1 / lead, ("E", n))
            else:
                part = chunks[n][2] / rows
                now += 0.06 * part
                if step < 5:
                    send(("core", "x", "z", "across", "back")[step], part, (step + 1, n))
            continue
        soon = min(pending.values()) if pending else 1e9
        if late:
            tap = late.pop(0)
            out.append(("g", tap))
            now += 0.7 if len(taps) - early_taps - len(late) <= 3 else 0.45
            free["core"] = max(free["core"], now) + core
            for n, chunk in enumerate(chunks):
                if chunk[0] == tap:
                    pending[1, n] = free["core"] + core_hop
            continue
        at = gate.get(filler[0], 0.0) if filler else 0.0
        waits = now < at
        if filler and not waits and (soon > now + SLACK or not pending):
            kind = filler.pop(0)
            out.append((kind, 0) if isinstance(kind, str) else ("i", kind))
            now += 0.3
        else:
            now = max(now, min(soon, at) if waits else soon)
    return out


def kernel(
    dims, lat, sav, og, tw, sw, ig_out, sums_out,
    savv, twv, twx, swv, opad, hid, savt, most, latl, lwide, latt, hs, acc, ig, gf, sums,
    gsend, g1, g2s, g2r, gz, gzf, gzr, qs, qf, qr, qown, qx,
    lsem, osend, orecv, osem, xsend, xrecv, bsem, ysem, lxsem, wysem, wzsend, wzrecv, wxsend, wxrecv, wcsem,
    s1s, s1r, s2s, s2r, s3s, s3r, isem, rsem, entered, qcore, qsem, qrecv, qxrecv,
):
    S, T, Z, F, Pl, Cl, Cs, scale, chunks, KT = dims
    U = S // 2
    HW = S * Pl
    C = T * Cl
    R = Pl // WS
    me_s, me_t, me_z = lax.axis_index("sp"), lax.axis_index("tp"), lax.axis_index("clip")
    me_u, me_c = me_s // 2, lax.rem(me_s, 2)
    sib = me_u * 2 + 1 - me_c
    far = (1 - me_u) * 2
    mate = (me_z, me_s, 1 - me_t)
    near = (me_z, sib, me_t)
    others = (sib, far + me_c, far + 1 - me_c)

    def remote(src, dst, send, recv, device):
        return pltpu.make_async_remote_copy(
            src_ref=src, dst_ref=dst, send_sem=send, recv_sem=recv, device_id=device, device_id_type=MESH
        )

    def block(n, base=0):
        return pl.ds(pl.multiple_of(base + n * Pl, 16), Pl)

    def window(n):
        at = jnp.clip(n * R - 1, 0, HW // WS - R - 2)
        return (
            pl.ds(pl.multiple_of(at * WS, WS), (R + 2) * WS),
            pl.ds(pl.multiple_of((at - n * R + 2) * WS, WS), (R + 2) * WS),
        )

    my_cols = pl.ds(pl.multiple_of(me_t * Cl, Cl), Cl)
    mate_cols = pl.ds(pl.multiple_of((1 - me_t) * Cl, Cl), Cl)
    loads = [
        pltpu.make_async_copy(src, dst, lsem.at[n]) for n, (src, dst) in enumerate(((tw, twv), (sav, savv), (sw, swv)))
    ]
    mine = [
        pltpu.make_async_copy(og.at[pl.ds(f * Pl, Pl)], opad.at[pl.ds((f + 1) * Pl, Pl), my_cols], osem)
        for f in range(F)
    ]
    own_og = pltpu.make_async_copy(og, opad.at[pl.ds(Pl, F * Pl), my_cols], osem)
    for f in range(F):
        latl[f, pl.ds(WS, WS), :] = jnp.zeros((WS, Cl), BF16)
        latl[f, pl.ds((R + 2) * WS, WS), :] = jnp.zeros((WS, Cl), BF16)
    for copy in mine + loads:
        copy.start()

    with scope("barrier"):
        barrier = pltpu.get_barrier_semaphore()
        peers = [mate, near, (me_z, others[1], me_t), (me_z, others[2], me_t)]
        first, last = me_z == 0, me_z == Z - 1
        count = len(peers) + jnp.where(jnp.logical_or(first, last), 1, 2)
        for peer in peers:
            pl.semaphore_signal(barrier, inc=1, device_id=peer, device_id_type=MESH)

        def tell(semaphore, step, sends):
            @pl.when(sends)
            def _():
                pl.semaphore_signal(
                    semaphore, inc=1, device_id=(jnp.clip(me_z + step, 0, Z - 1), me_s, me_t), device_id_type=MESH
                )

        tell(barrier, 1, jnp.logical_not(last))
        tell(barrier, -1, jnp.logical_not(first))
        pl.semaphore_wait(barrier, count)
        tell(entered.at[0], 1, me_z == 1)
        tell(entered.at[1], -1, me_z == Z - 2)

    def frame(k):
        return jnp.where(me_u == 0, F - 1 - k, k)

    share = Cl // (2 * Z * U)

    def slice_of(u, c, z):
        return twx.at[:, pl.ds(pl.multiple_of(((u * 2 + c) * Z + z) * share, 16), share)]

    def slices(n):
        return twx.at[:, pl.ds(0, n * share)]

    here = pl.ds(pl.multiple_of(((me_u * 2 + me_c) * Z + me_z) * share, 16), share)
    x_mate = (me_z, others[1], me_t)
    wy = remote(tw.at[:, here], twx.at[:, here], wysem.at[0], wysem.at[1], mate)
    wy.start()
    ocopies = []
    for k in range(F):
        f = frame(k)
        copy = remote(og.at[block(f)], opad.at[block(f, Pl), my_cols], osend, orecv.at[k], mate)
        copy.start()
        ocopies.append(copy)
    for n in (1, 2, 0):
        src, dst = window(others[n])
        remote(lat.at[src], latl.at[me_s, dst], lxsem.at[0], lxsem.at[1], (me_z, others[n], me_t)).start()
    src, dst = window(me_s)
    own = pltpu.make_async_copy(lat.at[src], latl.at[me_s, dst], lsem.at[3])
    own.start()

    opad[pl.ds(0, Pl), :] = jnp.zeros((Pl, C), BF16)
    opad[pl.ds((F + 1) * Pl, Pl), :] = jnp.zeros((Pl, C), BF16)
    for b in range(3):
        hs[b, pl.ds(0, WS), :] = jnp.zeros((WS, C), BF16)
        hs[b, pl.ds(WS + HW, WS), :] = jnp.zeros((WS, C), BF16)
    with scope("load"):
        own_og.wait()
        for copy in loads:
            copy.wait()
    savt[:, pl.ds(0, Pl)] = jnp.zeros((Cl, Pl), BF16)
    savt[:, pl.ds((F + 1) * Pl, Pl)] = jnp.zeros((Cl, Pl), BF16)
    savt[:, pl.ds(Pl, F * Pl)] = savv[...].T

    def pass_x(n):
        piece = slice_of(me_u, me_c, lax.rem(me_z + Z - n, Z))
        remote(piece, piece, wxsend, wxrecv.at[n], x_mate).start()
        remote(piece, piece, wcsem.at[0], wcsem.at[1], near).start()

    def pass_z(n):
        piece = slice_of(me_u, me_c, lax.rem(me_z + Z - n, Z))
        remote(piece, piece, wzsend, wzrecv.at[n - 1], (lax.rem(me_z + n, Z), me_s, me_t)).wait_recv()
        pass_x(n)

    def pass_core(n):
        piece = slice_of(1 - me_u, me_c, lax.rem(me_z + Z - n, Z))
        remote(piece, piece, wxsend, wxrecv.at[n], x_mate).wait_recv()
        remote(piece, piece, wcsem.at[0], wcsem.at[1], near).start()

    def hear(semaphore, step, hears, sends):
        @pl.when(hears)
        def _():
            pl.semaphore_wait(semaphore, 1)

        tell(semaphore, step, sends)

    with scope("wy"):
        wy.wait()
        hear(entered.at[0], 1, me_z >= 2, jnp.logical_and(me_z >= 2, me_z < Z - 1))
        hear(entered.at[1], -1, me_z <= Z - 3, jnp.logical_and(me_z <= Z - 3, me_z > 0))
    for dz in (1, Z - 1, 2):
        piece = slice_of(me_u, me_c, me_z)
        remote(piece, piece, wzsend, wzrecv.at[dz - 1], (lax.rem(me_z + dz, Z), me_s, me_t)).start()
    pass_x(0)

    with scope("passz"):
        pass_z(1)
        pass_z(Z - 1)
    with scope("lwait"):
        own.wait()
        part = lat.at[pl.ds(0, len(others) * (R + 2) * WS)]
        remote(part, part, lxsem.at[0], lxsem.at[1], near).wait()

    span = (R + 2) * WS
    column = lax.rem(lax.broadcasted_iota(jnp.int32, (span, Cl), 0), WS)

    def latents_of(f):
        lwide[...] = latl[f].astype(F32)
        for b in range(3):
            if b == 1:
                value = latl[f, pl.ds(WS, span), :]
            else:
                value = lwide[pl.ds(WS + b - 1, span), :]
                value = jnp.where(column != (WS - 1 if b == 2 else 0), value, 0.0).astype(BF16)
            for row in range(3):
                latt[3 * row + b, :, pl.ds(f * Pl, Pl)] = value[row * WS : row * WS + Pl].T

    def landing(n, part):
        at = pl.multiple_of(WS + n * Pl + part * (Pl // 2), 16)
        return hs.at[1, pl.ds(at, Pl // 2), my_cols]

    def send_block(k, parts=(0, 1)):
        f = frame(k)
        for part in parts:
            rows = pl.ds(pl.multiple_of(f * Pl + part * (Pl // 2), 16), Pl // 2)
            remote(
                hid.at[rows, my_cols], landing(me_s, part),
                xsend, xrecv.at[part, lax.rem(f + me_c, 2)], (me_z, f, me_t),
            ).start()

    def hidden(weights, at, size):
        total = None
        for k in range(KT):
            term = nt(opad[pl.ds(pl.multiple_of(at + (KT - 1 - k) * Pl, 16), size), :], weights[k])
            total = term if total is None else total + term
        return total.astype(BF16)

    arrived = 0

    def take(n):
        nonlocal arrived
        with scope(f"owait{n}"):
            while arrived < n:
                ocopies[arrived].wait_recv()
                arrived += 1

    for k in range(F - U):
        f = frame(k)
        if k == 0:
            with scope("lshift0"):
                for part_f in range(U):
                    latents_of(part_f)
            with scope("passz2"):
                pass_z(2)
        take(k + 2)
        with scope(f"hidden{k}"):
            hid[block(f), my_cols] = hidden(twv, f * Pl, Pl)
        send_block(k)
        if k == 0:
            with scope("lshift1"):
                for part_f in range(U, F):
                    latents_of(part_f)
    with scope("passc"):
        pass_core(0)
        pass_core(1)
    base = jnp.where(me_u == 0, U, 1)
    for tap in range(KT):
        with scope(f"p_{tap}"):
            at = pl.multiple_of((base + tap - 1) * Pl, 128)
            most[tap] = nn(
                savt[:, pl.ds(at, (F - 1) * Pl)], opad[pl.ds(pl.multiple_of(base * Pl, 16), (F - 1) * Pl), :]
            )
    take(F)

    sent = {}

    def view(n):
        tap, at, rows = chunks[n]
        return tap, pl.ds(at, rows)

    def start1(tap):
        sent[1, tap] = remote(gsend.at[1 - me_c, :, tap], g1.at[:, tap], s1s, s1r.at[tap], near)
        sent[1, tap].start()

    def step1(n):
        at = view(n)
        if (1, chunks[n][0]) in sent:
            sent.pop((1, chunks[n][0])).wait_recv()
        other = 1 - me_u
        g2s[at] = (gsend[(me_c, other) + at].astype(F32) + g1[(other,) + at].astype(F32)).astype(BF16)
        sent[2, n] = remote(g2s.at[at], g2r.at[at], s2s, s2r.at[n], (me_z, others[1], me_t))
        sent[2, n].start()

    half = Z // 2
    low = me_z < half
    is_end = jnp.logical_or(me_z == 0, me_z == Z - 1)
    is_inner = jnp.logical_or(me_z == half - 1, me_z == half)
    z_in = jnp.where(low, me_z + 1, me_z - 1)
    z_out = jnp.clip(jnp.where(low, me_z - 1, me_z + 1), 0, Z - 1)
    Z_INNER, Z_OUTER = 0, 1

    def hop(n, src, send, slot, target):
        at = view(n)
        return remote(src.at[at], gzr.at[(slot,) + at], s3s.at[send], s3r.at[slot, n], (target, me_s, me_t))

    def to_inner(n):
        return hop(n, gz, 0, Z_OUTER, z_in)

    def across(n):
        return hop(n, gz, 0, Z_INNER, z_in)

    def to_outer(n):
        return hop(n, gf, 1, Z_INNER, z_out)

    def result(n, value):
        at = view(n)
        sums[at] = value.astype(F32) * scale
        pltpu.make_async_copy(sums.at[at], sums_out.at[at], rsem).start()

    def step2(n):
        at = view(n)
        sent[2, n].wait_recv()
        total = gsend[(me_c, me_u) + at].astype(F32) + g1[(me_u,) + at].astype(F32)
        total = total + g2r[at].astype(F32)
        gzf[at] = total

        @pl.when(is_end)
        def _():
            gz[at] = total.astype(BF16)
            to_inner(n).start()

    def step3(n):
        at = view(n)

        @pl.when(is_inner)
        def _():
            to_inner(n).wait_recv()
            gz[at] = (gzf[at] + gzr[(Z_OUTER,) + at].astype(F32)).astype(BF16)
            across(n).start()

    def step4(n):
        at = view(n)

        @pl.when(is_inner)
        def _():
            across(n).wait_recv()
            value = (gz[at].astype(F32) + gzr[(Z_INNER,) + at].astype(F32)).astype(BF16)
            gf[at] = value
            to_outer(n).start()
            result(n, value)

    def step5(n):
        at = view(n)

        @pl.when(is_end)
        def _():
            across(n).wait_recv()
            result(n, gzr[(Z_INNER,) + at])

    def finish():
        remote(og, opad.at[pl.ds(Pl, F * Pl), my_cols], osend, orecv.at[0], mate).wait_send()
        part = hid.at[pl.ds(0, (F - U) * Pl), my_cols]
        remote(part, part, xsend, xrecv.at[0, 0], x_mate).wait_send()
        remote(slices(Z - 1), slices(Z - 1), wzsend, wzrecv.at[0], (z_in, me_s, me_t)).wait_send()
        remote(slices(Z), slices(Z), wxsend, wxrecv.at[0], x_mate).wait_send()
        remote(gsend.at[1 - me_c], g1, s1s, s1r.at[0], near).wait_send()
        remote(g2s, g2r, s2s, s2r.at[0], (me_z, others[1], me_t)).wait_send()
        rest = pl.ds(1, gz.shape[0] - 1)
        remote(gz.at[rest], gzr.at[Z_INNER, rest], s3s.at[0], s3r.at[0, 0], (z_in, me_s, me_t)).wait_send()
        remote(qs, qr.at[Z_INNER], qsem.at[0], qrecv.at[0, 0], (z_in, me_s, me_t)).wait_send()

        @pl.when(is_inner)
        def _():
            remote(gf.at[rest], gzr.at[Z_INNER, rest], s3s.at[1], s3r.at[0, 0], (z_out, me_s, me_t)).wait_send()
            remote(qf, qr.at[Z_INNER], qsem.at[1], qrecv.at[0, 0], (z_out, me_s, me_t)).wait_send()

        pltpu.make_async_copy(sums, sums_out, rsem).wait()

    def gradient(tap):
        if tap < KT:
            f = frame(F - 1)
            at = pl.multiple_of((f + tap) * Pl, 128)
            part = most[tap] + nn(savt[:, pl.ds(at, Pl)], opad[block(f, Pl), :])
        else:
            part = nn(latt[tap - KT], hid[...])
        for s in range(S):
            gsend[s % 2, s // 2, tap] = part[:, s * Cs : (s + 1) * Cs].astype(BF16)
        if tap:
            start1(tap)
        else:
            for n in range(LEADS):
                rows = lead_rows(n)
                remote(gsend.at[1 - me_c, :, 0, rows], g1.at[:, 0, rows], s1s, qcore.at[n], near).start()

    piece_rows = Cl // LEADS

    def lead_rows(n):
        return pl.ds(n * piece_rows, piece_rows)

    def lead_hop(n, src, send, slot, target):
        return remote(
            src.at[:, lead_rows(n)], qr.at[slot, :, lead_rows(n)], qsem.at[send], qrecv.at[slot, n],
            (target, me_s, me_t),
        )

    def lead_a(n):
        rows = lead_rows(n)
        remote(gsend.at[1 - me_c, :, 0, rows], g1.at[:, 0, rows], s1s, qcore.at[n], near).wait_recv()
        total = gsend[me_c, :, 0, rows].astype(F32) + g1[:, 0, rows].astype(F32)

        @pl.when(is_end)
        def _():
            qs[:, rows] = total.astype(BF16)
            lead_hop(n, qs, 0, Z_OUTER, z_in).start()

        @pl.when(is_inner)
        def _():
            qown[:, rows] = total

    def lead_b(n):
        rows = lead_rows(n)

        @pl.when(is_inner)
        def _():
            lead_hop(n, qs, 0, Z_OUTER, z_in).wait_recv()
            qs[:, rows] = (qown[:, rows] + qr[Z_OUTER, :, rows].astype(F32)).astype(BF16)
            lead_hop(n, qs, 0, Z_INNER, z_in).start()

    def lead_x(n, src):
        return remote(src.at[lead_rows(n)], qx.at[lead_rows(n)], s2s, qxrecv.at[n], x_mate)

    def lead_c(n):
        rows = lead_rows(n)

        @pl.when(is_inner)
        def _():
            lead_hop(n, qs, 0, Z_INNER, z_in).wait_recv()
            qf[:, rows] = (qs[:, rows].astype(F32) + qr[Z_INNER, :, rows].astype(F32)).astype(BF16)
            lead_hop(n, qf, 1, Z_INNER, z_out).start()
            lead_x(n, qf.at[1 - me_u]).start()

    def lead_d(n):
        @pl.when(is_end)
        def _():
            lead_hop(n, qs, 0, Z_INNER, z_in).wait_recv()
            lead_x(n, qr.at[Z_INNER, 1 - me_u]).start()

    def lead_e(n):
        rows = lead_rows(n)
        lead_x(n, qf.at[1 - me_u]).wait_recv()

        def done(mine):
            sums[0, rows] = (mine.astype(F32) + qx[rows].astype(F32)) * scale
            pltpu.make_async_copy(sums.at[0, rows], sums_out.at[0, rows], rsem).start()

        @pl.when(is_inner)
        def _():
            done(qf[me_u, rows])

        @pl.when(is_end)
        def _():
            done(qr[Z_INNER, me_u, rows])

    early = [n for n, chunk in enumerate(chunks) if chunk[0] < KT]
    for tap in range(KT):
        with scope(f"g_{tap}"):
            gradient(tap)
        if tap == 0:
            with scope("passd"):
                pass_core(Z - 1)
                pass_core(2)
    with scope("early0"):
        for n in range(LEADS):
            lead_a(n)
    with scope("hiddenown"):
        for k in range(F - U, F):
            f = frame(k)
            hid[block(f), my_cols] = hidden(twv, f * Pl, Pl)
    with scope("early"):
        for n in early:
            step1(n)
    with scope("wwait"):
        remote(slices(2 * Z), slices(2 * Z), wcsem.at[0], wcsem.at[1], near).wait()
    with scope("hiddenrest"):
        hid[:, mate_cols] = hidden(twx, 0, F * Pl)
    to_sib = remote(hid.at[block(sib)], hs.at[1, block(me_s, WS)], bsem.at[0], bsem.at[1], near)
    to_sib.start()
    def relay(part):
        for slot in range(2):
            piece = landing(others[1 + slot], part)
            remote(piece, piece, xsend, xrecv.at[part, slot], (me_z, others[1 + slot], me_t)).wait_recv()
            remote(piece, piece, ysem.at[0], ysem.at[1], mate).start()

    def arrive_near():
        to_sib.wait()
        hs[1, block(me_s, WS), :] = hid[block(me_s), :]
        shift(me_u * (HW // 2))

    def arrive_far():
        part = hs.at[1, pl.ds(pl.multiple_of(WS + far * Pl, 16), 2 * Pl), my_cols]
        remote(part, part, ysem.at[0], ysem.at[1], mate).wait()
        shift((1 - me_u) * (HW // 2))

    tile = 4 * WS

    def shift(base):
        column = lax.rem(lax.broadcasted_iota(jnp.int32, (tile, C), 0), WS)
        for r in range(0, HW // 2, tile):
            rows = pl.ds(pl.multiple_of(base + WS + r, WS), tile)
            value = hs[1, rows, :].astype(F32)
            for b in (-1, 1):
                keep = column != (0 if b == 1 else WS - 1)
                moved = pltpu.roll(value, 1 if b == 1 else tile - 1, 0)
                hs[b + 1, rows, :] = jnp.where(keep, moved, 0.0).astype(BF16)

    images = 2 * swv.shape[0]
    image_out = pltpu.make_async_copy(ig, ig_out, isem)
    near_rows, far_rows = HW // 2 - WS, HW // 2 + WS
    near_at = me_u * far_rows
    far_at = (1 - me_u) * near_rows

    def image(n):
        tap = n % (images // 2)
        row, col = tap // 3, tap % 3
        at, size = (near_at, near_rows) if n < images // 2 else (far_at, far_rows)
        rows = pl.ds(pl.multiple_of(at, WS), size)
        term = nt(hs[col, pl.ds(pl.multiple_of(at + (2 - row) * WS, WS), size), :], swv[tap])
        if tap == 0:
            acc[rows, :] = term
        elif tap < images // 2 - 1:
            acc[rows, :] += term
        else:
            ig[rows, :] = (acc[rows, :] + term).astype(BF16)
        if n == images - 1:
            image_out.start()

    steps = {"B": lead_b, "C": lead_c, "D": lead_d, "E": lead_e}
    steps |= {1: step1, 2: step2, 3: step3, 4: step4, 5: step5, "g": gradient, "i": image}
    for kind, n in order(chunks, LEADS, KT - 1, images, Cl):
        with scope(f"{kind}_{n}"):
            if kind == "r":
                relay(n)
            elif kind == "a":
                arrive_near()
            elif kind == "h":
                arrive_far()
            else:
                steps[kind](n)
    with scope("fin"):
        finish()
        image_out.wait()


def fused(sizes, latents, saved_input, out_grad, temporal_weight, spatial_weight):
    S, T, Z = sizes
    F, Pl, Cl = out_grad.shape[1:]
    KT, _, C = temporal_weight.shape
    taps = KT + spatial_weight.shape[0]
    HW = latents.shape[2]
    Cs = C // S
    U = S // 2
    scale = 1.0 / math.sqrt(Z * F * HS * WS)
    chunks = pieces_of(list(range(1, KT)) + [KT + tap for tap in FIRST], PARTS, Cl)
    N = len(chunks)
    dims = (S, T, Z, F, Pl, Cl, Cs, scale, chunks, KT)
    V = pltpu.VMEM
    D = pltpu.SemaphoreType.DMA
    hbm = pl.BlockSpec(memory_space=pltpu.HBM)
    vmem = pl.BlockSpec(memory_space=pltpu.VMEM)
    ig, sums = pl.pallas_call(
        functools.partial(kernel, dims),
        out_shape=(
            jax.ShapeDtypeStruct((HW, Cl), BF16),
            jax.ShapeDtypeStruct((taps, Cl, Cs), F32),
        ),
        in_specs=[hbm] * 5,
        out_specs=(pl.BlockSpec(memory_space=pl.ANY),) * 2,
        scratch_shapes=[
            V((F * Pl, Cl), BF16), V((KT, Cl, C), BF16), V((KT, Cl, C), BF16), V((taps - KT, Cl, C), BF16),
            V(((F + 2) * Pl, C), BF16), V((F * Pl, C), BF16), V((Cl, (F + 2) * Pl), BF16), V((KT, Cl, C), F32),
            V((F, Pl + 4 * WS, Cl), BF16), V((Pl + 4 * WS, Cl), F32), V((taps - KT, Cl, F * Pl), BF16),
            V((3, HW + 2 * WS, C), BF16), V((HW, Cl), F32),
            V((HW, Cl), BF16), V((taps, Cl, Cs), BF16), V((taps, Cl, Cs), F32),
            V((2, U, taps, Cl, Cs), BF16), V((U, taps, Cl, Cs), BF16), V((taps, Cl, Cs), BF16),
            V((taps, Cl, Cs), BF16), V((taps, Cl, Cs), BF16), V((taps, Cl, Cs), F32), V((2, taps, Cl, Cs), BF16),
            V((U, Cl, Cs), BF16), V((U, Cl, Cs), BF16), V((2, U, Cl, Cs), BF16), V((U, Cl, Cs), F32), V((Cl, Cs), BF16),
            D((4,)), D(()), D((F,)), D(()), D(()), D((2, 2)), D((2,)), D((2,)), D((2,)),
            D((2,)), D(()), D((Z - 1,)), D(()), D((Z,)), D((2,)),
            D(()), D((taps,)), D(()), D((N,)), D((2,)), D((2, N)), D(()), D(()), pltpu.SemaphoreType.REGULAR((2,)),
            D((LEADS,)), D((2,)), D((2, LEADS)), D((LEADS,)),
        ],
        compiler_params=pltpu.CompilerParams(
            collective_id=0, has_side_effects=True, vmem_limit_bytes=44 * 2**20
        ),
    )(*(
        pltpu.with_memory_space_constraint(value, pltpu.HBM)
        for value in (
            latents.reshape(HW, Cl), saved_input.reshape(F * Pl, Cl), out_grad.reshape(F * Pl, Cl),
            temporal_weight, spatial_weight,
        )
    ))

    def finish(ig_ref, sums_ref, ig_out, tg_out, sg_out, sem):
        half = (taps - KT) // 2
        pairs = (
            (sums_ref.at[pl.ds(KT, half)], sg_out.at[pl.ds(0, half)]),
            (sums_ref.at[pl.ds(KT + half, taps - KT - half)], sg_out.at[pl.ds(half, taps - KT - half)]),
            (sums_ref.at[pl.ds(0, KT)], tg_out),
            (ig_ref, ig_out),
        )
        copies = [pltpu.make_async_copy(src, dst, sem.at[n]) for n, (src, dst) in enumerate(pairs)]
        for copy in copies:
            copy.start()
        for copy in copies:
            copy.wait()

    ig, tg, sg = pl.pallas_call(
        finish,
        out_shape=(
            jax.ShapeDtypeStruct((HW, Cl), BF16),
            jax.ShapeDtypeStruct((KT, Cl, Cs), F32),
            jax.ShapeDtypeStruct((taps - KT, Cl, Cs), F32),
        ),
        in_specs=[vmem] * 2,
        out_specs=(hbm,) * 3,
        scratch_shapes=[D((4,))],
        compiler_params=pltpu.CompilerParams(vmem_limit_bytes=16 * 2**20),
    )(ig, sums)
    return ig.reshape(latents.shape), tg, sg


def plain(latents, saved_input, out_grad, temporal_weight, spatial_weight):
    clips_all = latents.shape[0] * lax.axis_size("clip")
    frames_all = latents.shape[1] * lax.axis_size("sp")
    scale_factor = 1.0 / math.sqrt(clips_all * frames_all * HS * WS)
    frames_count = out_grad.shape[1]
    local_in = temporal_weight.shape[1]
    saved_padded = pad_frames(saved_input)
    block_in = lax.all_gather(out_grad, "tp", axis=3, tiled=True)
    padded = pad_frames(block_in)
    hidden_acc = jnp.zeros(out_grad.shape[:3] + (local_in,), F32)
    parts = []
    for tap_index in range(3):
        shifted = padded[:, 2 - tap_index : 2 - tap_index + frames_count]
        hidden_acc = hidden_acc + jnp.einsum(
            "bfpo,io->bfpi", shifted, temporal_weight[tap_index], preferred_element_type=F32
        )
        window = saved_padded[:, tap_index : tap_index + frames_count]
        parts.append(jnp.einsum("bfpi,bfpo->io", window, block_in, preferred_element_type=F32))
    temporal_local = jnp.stack(parts)
    hidden_grad = hidden_acc.astype(BF16)
    regrouped = lax.all_to_all(hidden_grad, "sp", split_axis=1, concat_axis=2, tiled=True)
    batch = latents.shape[0] * latents.shape[1]
    image_pad = jnp.pad(latents.reshape(batch, HS, WS, local_in), ((0, 0), (1, 1), (1, 1), (0, 0)))
    block_in = lax.all_gather(regrouped, "tp", axis=3, tiled=True)
    whole = block_in.reshape(batch, HS, WS, block_in.shape[3])
    grid = jnp.pad(whole, ((0, 0), (1, 1), (1, 1), (0, 0)))
    input_acc = jnp.zeros((batch, HS, WS, local_in), F32)
    parts = []
    for row in (-1, 0, 1):
        for col in (-1, 0, 1):
            tap_index = 3 * (row + 1) + (col + 1)
            moved = grid[:, 1 - row : 1 - row + HS, 1 - col : 1 - col + WS]
            input_acc = input_acc + jnp.einsum(
                "gabo,co->gabc", moved, spatial_weight[tap_index], preferred_element_type=F32
            )
            window = image_pad[:, 1 + row : 1 + row + HS, 1 + col : 1 + col + WS]
            parts.append(jnp.einsum("gabc,gabo->co", window, whole, preferred_element_type=F32))
    spatial_local = jnp.stack(parts)
    input_grad = input_acc.reshape(latents.shape).astype(BF16)
    temporal_grad, spatial_grad = lax.psum(
        tuple(
            lax.psum_scatter(value * scale_factor, "sp", scatter_dimension=2, tiled=True)
            for value in (temporal_local, spatial_local)
        ),
        "clip",
    )
    return input_grad, temporal_grad, spatial_grad


PARTS = [4, 4, 2, 2, 2, 2, 2, 2, 2, 2, 4]
HOP = 2.1
START = -0.6
LEAD = -2.6
LEADS = 4
NEAR = 3.0
EARLY = 1.5
SLACK = 0.25
LATE = {5: 3.0, "E": 2.0}
FIRST = [4, 3, 5, 0, 1, 2, 6, 7, 8]


def solution(mesh):
    sizes = (mesh.shape["sp"], mesh.shape["tp"], mesh.shape["clip"])

    def local(latents, saved_input, out_grad, temporal_weight, spatial_weight):
        S, T, Z = sizes
        cols = temporal_weight.shape[2] // S
        fits = (
            latents.shape[:2] == (1, 1) and S == out_grad.shape[1] == 4 and T == 2 and Z == 4
            and cols % 128 == 0 and out_grad.shape[3] % 256 == 0 and out_grad.shape[2] % 128 == 0
            and latents.shape[2] == HS * WS == S * out_grad.shape[2]
        )
        args = (latents, saved_input, out_grad, temporal_weight, spatial_weight)
        return fused(sizes, *args) if fits else plain(*args)

    return jax.shard_map(
        local,
        mesh=mesh,
        in_specs=(
            P("clip", "sp", None, "tp"),
            P("clip", None, "sp", "tp"),
            P("clip", None, "sp", "tp"),
            P(None, "tp", None),
            P(None, "tp", None),
        ),
        out_specs=(P("clip", "sp", None, "tp"), P(None, "tp", "sp"), P(None, "tp", "sp")),
        check_vma=False,
    )
```

```python
import contextlib
import functools
import math

import jax
import jax.numpy as jnp
from jax import lax
from jax.experimental import pallas as pl
from jax.experimental.pallas import tpu as pltpu
from jax.sharding import PartitionSpec as P

HS = 32
WS = 32
MESH = pl.DeviceIdType.MESH
F32 = jnp.float32
BF16 = jnp.bfloat16


def pad_frames(values):
    return jnp.pad(values, ((0, 0), (1, 1), (0, 0), (0, 0)))


def nt(a, b):
    return lax.dot_general(a, b, (((1,), (1,)), ((), ())), preferred_element_type=F32)


def nn(a, b):
    return lax.dot_general(a, b, (((1,), (0,)), ((), ())), preferred_element_type=F32)


scope = contextlib.nullcontext


def pieces_of(taps, parts, rows):
    return [(tap, part * (rows // n), rows // n) for tap, n in zip(taps, parts) for part in range(n)]


def order(chunks, lead, early_taps, images, rows):
    hop, core_hop, link, core = HOP, 0.65, 1.39, 0.44
    now, free = START, {"core": 0.0, "x": START, "z": LEAD, "across": 0.0, "back": 0.0}
    pending, out = {}, []

    def send(name, part, key, step=None):
        free[name] = max(free[name], now) + (core if name == "core" else link) * part
        pending[key] = free[name] + (core_hop if name == "core" else hop) + LATE.get(key[0], 0.0)

    taps = list(dict.fromkeys(tap for tap, _, _ in chunks))
    late = taps[early_taps:]
    filler = ["a"] + list(range(images // 2)) + ["h"] + list(range(images // 2, images))
    for n, chunk in enumerate(chunks):
        if chunk[0] not in late:
            send("x", chunk[2] / rows, (2, n))
    now = LEAD
    for n in range(lead):
        send("z", 2 / lead, ("B", n))
    now = 0.0
    gate = {"a": NEAR, "h": 1e9}
    pending["r", 0], pending["r", 1] = EARLY, EARLY + 1.4
    while pending or late or filler:
        ready = sorted((at, str(key), key) for key, at in pending.items() if at <= now)
        if ready:
            at, _, (step, n) = ready[0]
            del pending[step, n]
            out.append((step, n))
            if step == "r":
                now += 0.05
                gate["h"] = now + 2.5 * link + hop if n else gate["h"]
            elif isinstance(step, str):
                now += 0.05
                if step == "B":
                    send("across", 2 / lead, ("C", n))
                elif step == "C":
                    send("back", 2 / lead, ("D", n))
                elif step == "D":
                    send("x", 1 / lead, ("E", n))
            else:
                part = chunks[n][2] / rows
                now += 0.06 * part
                if step < 5:
                    send(("core", "x", "z", "across", "back")[step], part, (step + 1, n))
            continue
        soon = min(pending.values()) if pending else 1e9
        if late:
            tap = late.pop(0)
            out.append(("g", tap))
            now += 0.7 if len(taps) - early_taps - len(late) <= 3 else 0.45
            for n, chunk in enumerate(chunks):
                if chunk[0] == tap:
                    send("core", chunk[2] / rows, (1, n))
            continue
        at = gate.get(filler[0], 0.0) if filler else 0.0
        waits = now < at
        if filler and not waits and (soon > now + SLACK or not pending):
            kind = filler.pop(0)
            out.append((kind, 0) if isinstance(kind, str) else ("i", kind))
            now += 0.3
        else:
            now = max(now, min(soon, at) if waits else soon)
    return out


def kernel(
    dims, lat, sav, og, tw, sw, ig_out, sums_out,
    savv, twv, twx, swv, opad, hid, savt, most, latl, lwide, latt, hs, acc, ig, gf, sums,
    gsend, g1, g2s, g2r, gz, gzf, gzr, qs, qf, qr, qown, qx,
    lsem, osend, orecv, osem, xsend, xrecv, bsem, ysem, lxsem, wysem, wzsend, wzrecv, wxsend, wxrecv, wcsem,
    s1s, s1r, s2s, s2r, s3s, s3r, isem, rsem, entered, qcore, qsem, qrecv, qxrecv,
):
    S, T, Z, F, Pl, Cl, Cs, scale, chunks, KT = dims
    U = S // 2
    HW = S * Pl
    C = T * Cl
    R = Pl // WS
    me_s, me_t, me_z = lax.axis_index("sp"), lax.axis_index("tp"), lax.axis_index("clip")
    me_u, me_c = me_s // 2, lax.rem(me_s, 2)
    sib = me_u * 2 + 1 - me_c
    far = (1 - me_u) * 2
    mate = (me_z, me_s, 1 - me_t)
    near = (me_z, sib, me_t)
    others = (sib, far + me_c, far + 1 - me_c)

    def remote(src, dst, send, recv, device):
        return pltpu.make_async_remote_copy(
            src_ref=src, dst_ref=dst, send_sem=send, recv_sem=recv, device_id=device, device_id_type=MESH
        )

    def block(n, base=0):
        return pl.ds(pl.multiple_of(base + n * Pl, 16), Pl)

    def window(n):
        at = jnp.clip(n * R - 1, 0, HW // WS - R - 2)
        return (
            pl.ds(pl.multiple_of(at * WS, WS), (R + 2) * WS),
            pl.ds(pl.multiple_of((at - n * R + 2) * WS, WS), (R + 2) * WS),
        )

    my_cols = pl.ds(pl.multiple_of(me_t * Cl, Cl), Cl)
    mate_cols = pl.ds(pl.multiple_of((1 - me_t) * Cl, Cl), Cl)
    loads = [
        pltpu.make_async_copy(src, dst, lsem.at[n]) for n, (src, dst) in enumerate(((tw, twv), (sav, savv), (sw, swv)))
    ]
    mine = [
        pltpu.make_async_copy(og.at[pl.ds(f * Pl, Pl)], opad.at[pl.ds((f + 1) * Pl, Pl), my_cols], osem)
        for f in range(F)
    ]
    own_og = pltpu.make_async_copy(og, opad.at[pl.ds(Pl, F * Pl), my_cols], osem)
    for f in range(F):
        latl[f, pl.ds(WS, WS), :] = jnp.zeros((WS, Cl), BF16)
        latl[f, pl.ds((R + 2) * WS, WS), :] = jnp.zeros((WS, Cl), BF16)
    for copy in mine + loads:
        copy.start()

    with scope("barrier"):
        barrier = pltpu.get_barrier_semaphore()
        peers = [mate, near, (me_z, others[1], me_t), (me_z, others[2], me_t)]
        first, last = me_z == 0, me_z == Z - 1
        count = len(peers) + jnp.where(jnp.logical_or(first, last), 1, 2)
        for peer in peers:
            pl.semaphore_signal(barrier, inc=1, device_id=peer, device_id_type=MESH)

        def tell(semaphore, step, sends):
            @pl.when(sends)
            def _():
                pl.semaphore_signal(
                    semaphore, inc=1, device_id=(jnp.clip(me_z + step, 0, Z - 1), me_s, me_t), device_id_type=MESH
                )

        tell(barrier, 1, jnp.logical_not(last))
        tell(barrier, -1, jnp.logical_not(first))
        pl.semaphore_wait(barrier, count)
        tell(entered.at[0], 1, me_z == 1)
        tell(entered.at[1], -1, me_z == Z - 2)

    def frame(k):
        return jnp.where(me_u == 0, F - 1 - k, k)

    share = Cl // (2 * Z * U)

    def slice_of(u, c, z):
        return twx.at[:, pl.ds(pl.multiple_of(((u * 2 + c) * Z + z) * share, 16), share)]

    def slices(n):
        return twx.at[:, pl.ds(0, n * share)]

    here = pl.ds(pl.multiple_of(((me_u * 2 + me_c) * Z + me_z) * share, 16), share)
    x_mate = (me_z, others[1], me_t)
    wy = remote(tw.at[:, here], twx.at[:, here], wysem.at[0], wysem.at[1], mate)
    wy.start()
    ocopies = []
    for k in range(F):
        f = frame(k)
        copy = remote(og.at[block(f)], opad.at[block(f, Pl), my_cols], osend, orecv.at[k], mate)
        copy.start()
        ocopies.append(copy)
    for n in (1, 2, 0):
        src, dst = window(others[n])
        remote(lat.at[src], latl.at[me_s, dst], lxsem.at[0], lxsem.at[1], (me_z, others[n], me_t)).start()
    src, dst = window(me_s)
    own = pltpu.make_async_copy(lat.at[src], latl.at[me_s, dst], lsem.at[3])
    own.start()

    opad[pl.ds(0, Pl), :] = jnp.zeros((Pl, C), BF16)
    opad[pl.ds((F + 1) * Pl, Pl), :] = jnp.zeros((Pl, C), BF16)
    for b in range(3):
        hs[b, pl.ds(0, WS), :] = jnp.zeros((WS, C), BF16)
        hs[b, pl.ds(WS + HW, WS), :] = jnp.zeros((WS, C), BF16)
    with scope("load"):
        own_og.wait()
        for copy in loads:
            copy.wait()
    savt[:, pl.ds(0, Pl)] = jnp.zeros((Cl, Pl), BF16)
    savt[:, pl.ds((F + 1) * Pl, Pl)] = jnp.zeros((Cl, Pl), BF16)
    savt[:, pl.ds(Pl, F * Pl)] = savv[...].T

    def pass_x(n):
        piece = slice_of(me_u, me_c, lax.rem(me_z + Z - n, Z))
        remote(piece, piece, wxsend, wxrecv.at[n], x_mate).start()
        remote(piece, piece, wcsem.at[0], wcsem.at[1], near).start()

    def pass_z(n):
        piece = slice_of(me_u, me_c, lax.rem(me_z + Z - n, Z))
        remote(piece, piece, wzsend, wzrecv.at[n - 1], (lax.rem(me_z + n, Z), me_s, me_t)).wait_recv()
        pass_x(n)

    def pass_core(n):
        piece = slice_of(1 - me_u, me_c, lax.rem(me_z + Z - n, Z))
        remote(piece, piece, wxsend, wxrecv.at[n], x_mate).wait_recv()
        remote(piece, piece, wcsem.at[0], wcsem.at[1], near).start()

    def hear(semaphore, step, hears, sends):
        @pl.when(hears)
        def _():
            pl.semaphore_wait(semaphore, 1)

        tell(semaphore, step, sends)

    with scope("wy"):
        wy.wait()
        hear(entered.at[0], 1, me_z >= 2, jnp.logical_and(me_z >= 2, me_z < Z - 1))
        hear(entered.at[1], -1, me_z <= Z - 3, jnp.logical_and(me_z <= Z - 3, me_z > 0))
    for dz in (1, Z - 1, 2):
        piece = slice_of(me_u, me_c, me_z)
        remote(piece, piece, wzsend, wzrecv.at[dz - 1], (lax.rem(me_z + dz, Z), me_s, me_t)).start()
    pass_x(0)

    with scope("passz"):
        pass_z(1)
        pass_z(Z - 1)
    with scope("lwait"):
        own.wait()
        part = lat.at[pl.ds(0, len(others) * (R + 2) * WS)]
        remote(part, part, lxsem.at[0], lxsem.at[1], near).wait()

    span = (R + 2) * WS
    column = lax.rem(lax.broadcasted_iota(jnp.int32, (span, Cl), 0), WS)

    def latents_of(f):
        lwide[...] = latl[f].astype(F32)
        for b in range(3):
            if b == 1:
                value = latl[f, pl.ds(WS, span), :]
            else:
                value = lwide[pl.ds(WS + b - 1, span), :]
                value = jnp.where(column != (WS - 1 if b == 2 else 0), value, 0.0).astype(BF16)
            for row in range(3):
                latt[3 * row + b, :, pl.ds(f * Pl, Pl)] = value[row * WS : row * WS + Pl].T

    def landing(n, part):
        at = pl.multiple_of(WS + n * Pl + part * (Pl // 2), 16)
        return hs.at[1, pl.ds(at, Pl // 2), my_cols]

    def send_block(k, parts=(0, 1)):
        f = frame(k)
        for part in parts:
            rows = pl.ds(pl.multiple_of(f * Pl + part * (Pl // 2), 16), Pl // 2)
            remote(
                hid.at[rows, my_cols], landing(me_s, part),
                xsend, xrecv.at[part, lax.rem(f + me_c, 2)], (me_z, f, me_t),
            ).start()

    def hidden(weights, at, size):
        total = None
        for k in range(KT):
            term = nt(opad[pl.ds(pl.multiple_of(at + (KT - 1 - k) * Pl, 16), size), :], weights[k])
            total = term if total is None else total + term
        return total.astype(BF16)

    arrived = 0

    def take(n):
        nonlocal arrived
        with scope(f"owait{n}"):
            while arrived < n:
                ocopies[arrived].wait_recv()
                arrived += 1

    for k in range(F - U):
        f = frame(k)
        if k == 0:
            with scope("lshift0"):
                for part_f in range(U):
                    latents_of(part_f)
            with scope("passz2"):
                pass_z(2)
        take(k + 2)
        with scope(f"hidden{k}"):
            hid[block(f), my_cols] = hidden(twv, f * Pl, Pl)
        send_block(k)
        if k == 0:
            with scope("lshift1"):
                for part_f in range(U, F):
                    latents_of(part_f)
    with scope("passc"):
        pass_core(0)
        pass_core(1)
    base = jnp.where(me_u == 0, U, 1)
    for tap in range(KT):
        with scope(f"p_{tap}"):
            at = pl.multiple_of((base + tap - 1) * Pl, 128)
            most[tap] = nn(
                savt[:, pl.ds(at, (F - 1) * Pl)], opad[pl.ds(pl.multiple_of(base * Pl, 16), (F - 1) * Pl), :]
            )
    take(F)

    sent = {}

    def view(n):
        tap, at, rows = chunks[n]
        return tap, pl.ds(at, rows)

    def start1(n):
        at = view(n)
        sent[1, n] = remote(gsend.at[(1 - me_c, slice(None)) + at], g1.at[(slice(None),) + at], s1s, s1r.at[n], near)
        sent[1, n].start()

    def step1(n):
        at = view(n)
        sent[1, n].wait_recv()
        other = 1 - me_u
        g2s[at] = (gsend[(me_c, other) + at].astype(F32) + g1[(other,) + at].astype(F32)).astype(BF16)
        sent[2, n] = remote(g2s.at[at], g2r.at[at], s2s, s2r.at[n], (me_z, others[1], me_t))
        sent[2, n].start()

    half = Z // 2
    low = me_z < half
    is_end = jnp.logical_or(me_z == 0, me_z == Z - 1)
    is_inner = jnp.logical_or(me_z == half - 1, me_z == half)
    z_in = jnp.where(low, me_z + 1, me_z - 1)
    z_out = jnp.clip(jnp.where(low, me_z - 1, me_z + 1), 0, Z - 1)
    Z_INNER, Z_OUTER = 0, 1

    def hop(n, src, send, slot, target):
        at = view(n)
        return remote(src.at[at], gzr.at[(slot,) + at], s3s.at[send], s3r.at[slot, n], (target, me_s, me_t))

    def to_inner(n):
        return hop(n, gz, 0, Z_OUTER, z_in)

    def across(n):
        return hop(n, gz, 0, Z_INNER, z_in)

    def to_outer(n):
        return hop(n, gf, 1, Z_INNER, z_out)

    def result(n, value):
        at = view(n)
        sums[at] = value.astype(F32) * scale
        pltpu.make_async_copy(sums.at[at], sums_out.at[at], rsem).start()

    def step2(n):
        at = view(n)
        sent[2, n].wait_recv()
        total = gsend[(me_c, me_u) + at].astype(F32) + g1[(me_u,) + at].astype(F32)
        total = total + g2r[at].astype(F32)
        gzf[at] = total

        @pl.when(is_end)
        def _():
            gz[at] = total.astype(BF16)
            to_inner(n).start()

    def step3(n):
        at = view(n)

        @pl.when(is_inner)
        def _():
            to_inner(n).wait_recv()
            gz[at] = (gzf[at] + gzr[(Z_OUTER,) + at].astype(F32)).astype(BF16)
            across(n).start()

    def step4(n):
        at = view(n)

        @pl.when(is_inner)
        def _():
            across(n).wait_recv()
            value = (gz[at].astype(F32) + gzr[(Z_INNER,) + at].astype(F32)).astype(BF16)
            gf[at] = value
            to_outer(n).start()
            result(n, value)

    def step5(n):
        at = view(n)

        @pl.when(is_end)
        def _():
            across(n).wait_recv()
            result(n, gzr[(Z_INNER,) + at])

    def finish():
        remote(og, opad.at[pl.ds(Pl, F * Pl), my_cols], osend, orecv.at[0], mate).wait_send()
        part = hid.at[pl.ds(0, (F - U) * Pl), my_cols]
        remote(part, part, xsend, xrecv.at[0, 0], x_mate).wait_send()
        remote(slices(Z - 1), slices(Z - 1), wzsend, wzrecv.at[0], (z_in, me_s, me_t)).wait_send()
        remote(slices(Z), slices(Z), wxsend, wxrecv.at[0], x_mate).wait_send()
        remote(gsend.at[1 - me_c], g1, s1s, s1r.at[0], near).wait_send()
        remote(g2s, g2r, s2s, s2r.at[0], (me_z, others[1], me_t)).wait_send()
        rest = pl.ds(1, gz.shape[0] - 1)
        remote(gz.at[rest], gzr.at[Z_INNER, rest], s3s.at[0], s3r.at[0, 0], (z_in, me_s, me_t)).wait_send()
        remote(qs, qr.at[Z_INNER], qsem.at[0], qrecv.at[0, 0], (z_in, me_s, me_t)).wait_send()

        @pl.when(is_inner)
        def _():
            remote(gf.at[rest], gzr.at[Z_INNER, rest], s3s.at[1], s3r.at[0, 0], (z_out, me_s, me_t)).wait_send()
            remote(qf, qr.at[Z_INNER], qsem.at[1], qrecv.at[0, 0], (z_out, me_s, me_t)).wait_send()

        pltpu.make_async_copy(sums, sums_out, rsem).wait()

    def gradient(tap):
        if tap < KT:
            f = frame(F - 1)
            at = pl.multiple_of((f + tap) * Pl, 128)
            part = most[tap] + nn(savt[:, pl.ds(at, Pl)], opad[block(f, Pl), :])
        else:
            part = nn(latt[tap - KT], hid[...])
        for s in range(S):
            gsend[s % 2, s // 2, tap] = part[:, s * Cs : (s + 1) * Cs].astype(BF16)
        for n, chunk in enumerate(chunks):
            if chunk[0] == tap:
                start1(n)
        if tap == 0:
            for n in range(LEADS):
                rows = lead_rows(n)
                remote(gsend.at[1 - me_c, :, 0, rows], g1.at[:, 0, rows], s1s, qcore.at[n], near).start()

    piece_rows = Cl // LEADS

    def lead_rows(n):
        return pl.ds(n * piece_rows, piece_rows)

    def lead_hop(n, src, send, slot, target):
        return remote(
            src.at[:, lead_rows(n)], qr.at[slot, :, lead_rows(n)], qsem.at[send], qrecv.at[slot, n],
            (target, me_s, me_t),
        )

    def lead_a(n):
        rows = lead_rows(n)
        remote(gsend.at[1 - me_c, :, 0, rows], g1.at[:, 0, rows], s1s, qcore.at[n], near).wait_recv()
        total = gsend[me_c, :, 0, rows].astype(F32) + g1[:, 0, rows].astype(F32)

        @pl.when(is_end)
        def _():
            qs[:, rows] = total.astype(BF16)
            lead_hop(n, qs, 0, Z_OUTER, z_in).start()

        @pl.when(is_inner)
        def _():
            qown[:, rows] = total

    def lead_b(n):
        rows = lead_rows(n)

        @pl.when(is_inner)
        def _():
            lead_hop(n, qs, 0, Z_OUTER, z_in).wait_recv()
            qs[:, rows] = (qown[:, rows] + qr[Z_OUTER, :, rows].astype(F32)).astype(BF16)
            lead_hop(n, qs, 0, Z_INNER, z_in).start()

    def lead_x(n, src):
        return remote(src.at[lead_rows(n)], qx.at[lead_rows(n)], s2s, qxrecv.at[n], x_mate)

    def lead_c(n):
        rows = lead_rows(n)

        @pl.when(is_inner)
        def _():
            lead_hop(n, qs, 0, Z_INNER, z_in).wait_recv()
            qf[:, rows] = (qs[:, rows].astype(F32) + qr[Z_INNER, :, rows].astype(F32)).astype(BF16)
            lead_hop(n, qf, 1, Z_INNER, z_out).start()
            lead_x(n, qf.at[1 - me_u]).start()

    def lead_d(n):
        @pl.when(is_end)
        def _():
            lead_hop(n, qs, 0, Z_INNER, z_in).wait_recv()
            lead_x(n, qr.at[Z_INNER, 1 - me_u]).start()

    def lead_e(n):
        rows = lead_rows(n)
        lead_x(n, qf.at[1 - me_u]).wait_recv()

        def done(mine):
            sums[0, rows] = (mine.astype(F32) + qx[rows].astype(F32)) * scale
            pltpu.make_async_copy(sums.at[0, rows], sums_out.at[0, rows], rsem).start()

        @pl.when(is_inner)
        def _():
            done(qf[me_u, rows])

        @pl.when(is_end)
        def _():
            done(qr[Z_INNER, me_u, rows])

    early = [n for n, chunk in enumerate(chunks) if chunk[0] < KT]
    for tap in range(KT):
        with scope(f"g_{tap}"):
            gradient(tap)
        if tap == 0:
            with scope("passd"):
                pass_core(Z - 1)
                pass_core(2)
    with scope("early0"):
        for n in range(LEADS):
            lead_a(n)
    with scope("hiddenown"):
        for k in range(F - U, F):
            f = frame(k)
            hid[block(f), my_cols] = hidden(twv, f * Pl, Pl)
    with scope("early"):
        for n in early:
            step1(n)
    with scope("wwait"):
        remote(slices(2 * Z), slices(2 * Z), wcsem.at[0], wcsem.at[1], near).wait()
    with scope("hiddenrest"):
        hid[:, mate_cols] = hidden(twx, 0, F * Pl)
    to_sib = remote(hid.at[block(sib)], hs.at[1, block(me_s, WS)], bsem.at[0], bsem.at[1], near)
    to_sib.start()
    def relay(part):
        for slot in range(2):
            piece = landing(others[1 + slot], part)
            remote(piece, piece, xsend, xrecv.at[part, slot], (me_z, others[1 + slot], me_t)).wait_recv()
            remote(piece, piece, ysem.at[0], ysem.at[1], mate).start()

    def arrive_near():
        to_sib.wait()
        hs[1, block(me_s, WS), :] = hid[block(me_s), :]
        shift(me_u * (HW // 2))

    def arrive_far():
        part = hs.at[1, pl.ds(pl.multiple_of(WS + far * Pl, 16), 2 * Pl), my_cols]
        remote(part, part, ysem.at[0], ysem.at[1], mate).wait()
        shift((1 - me_u) * (HW // 2))

    tile = 4 * WS

    def shift(base):
        column = lax.rem(lax.broadcasted_iota(jnp.int32, (tile, C), 0), WS)
        for r in range(0, HW // 2, tile):
            rows = pl.ds(pl.multiple_of(base + WS + r, WS), tile)
            value = hs[1, rows, :].astype(F32)
            for b in (-1, 1):
                keep = column != (0 if b == 1 else WS - 1)
                moved = pltpu.roll(value, 1 if b == 1 else tile - 1, 0)
                hs[b + 1, rows, :] = jnp.where(keep, moved, 0.0).astype(BF16)

    images = 2 * swv.shape[0]
    image_out = pltpu.make_async_copy(ig, ig_out, isem)
    near_rows, far_rows = HW // 2 - WS, HW // 2 + WS
    near_at = me_u * far_rows
    far_at = (1 - me_u) * near_rows

    def image(n):
        tap = n % (images // 2)
        row, col = tap // 3, tap % 3
        at, size = (near_at, near_rows) if n < images // 2 else (far_at, far_rows)
        rows = pl.ds(pl.multiple_of(at, WS), size)
        term = nt(hs[col, pl.ds(pl.multiple_of(at + (2 - row) * WS, WS), size), :], swv[tap])
        if tap == 0:
            acc[rows, :] = term
        elif tap < images // 2 - 1:
            acc[rows, :] += term
        else:
            ig[rows, :] = (acc[rows, :] + term).astype(BF16)
        if n == images - 1:
            image_out.start()

    steps = {"B": lead_b, "C": lead_c, "D": lead_d, "E": lead_e}
    steps |= {1: step1, 2: step2, 3: step3, 4: step4, 5: step5, "g": gradient, "i": image}
    for kind, n in order(chunks, LEADS, KT - 1, images, Cl):
        with scope(f"{kind}_{n}"):
            if kind == "r":
                relay(n)
            elif kind == "a":
                arrive_near()
            elif kind == "h":
                arrive_far()
            else:
                steps[kind](n)
    with scope("fin"):
        finish()
        image_out.wait()


def fused(sizes, latents, saved_input, out_grad, temporal_weight, spatial_weight):
    S, T, Z = sizes
    F, Pl, Cl = out_grad.shape[1:]
    KT, _, C = temporal_weight.shape
    taps = KT + spatial_weight.shape[0]
    HW = latents.shape[2]
    Cs = C // S
    U = S // 2
    scale = 1.0 / math.sqrt(Z * F * HS * WS)
    chunks = pieces_of(list(range(1, KT)) + [KT + tap for tap in FIRST], PARTS, Cl)
    N = len(chunks)
    dims = (S, T, Z, F, Pl, Cl, Cs, scale, chunks, KT)
    V = pltpu.VMEM
    D = pltpu.SemaphoreType.DMA
    hbm = pl.BlockSpec(memory_space=pltpu.HBM)
    vmem = pl.BlockSpec(memory_space=pltpu.VMEM)
    ig, sums = pl.pallas_call(
        functools.partial(kernel, dims),
        out_shape=(
            jax.ShapeDtypeStruct((HW, Cl), BF16),
            jax.ShapeDtypeStruct((taps, Cl, Cs), F32),
        ),
        in_specs=[hbm] * 5,
        out_specs=(pl.BlockSpec(memory_space=pl.ANY),) * 2,
        scratch_shapes=[
            V((F * Pl, Cl), BF16), V((KT, Cl, C), BF16), V((KT, Cl, C), BF16), V((taps - KT, Cl, C), BF16),
            V(((F + 2) * Pl, C), BF16), V((F * Pl, C), BF16), V((Cl, (F + 2) * Pl), BF16), V((KT, Cl, C), F32),
            V((F, Pl + 4 * WS, Cl), BF16), V((Pl + 4 * WS, Cl), F32), V((taps - KT, Cl, F * Pl), BF16),
            V((3, HW + 2 * WS, C), BF16), V((HW, Cl), F32),
            V((HW, Cl), BF16), V((taps, Cl, Cs), BF16), V((taps, Cl, Cs), F32),
            V((2, U, taps, Cl, Cs), BF16), V((U, taps, Cl, Cs), BF16), V((taps, Cl, Cs), BF16),
            V((taps, Cl, Cs), BF16), V((taps, Cl, Cs), BF16), V((taps, Cl, Cs), F32), V((2, taps, Cl, Cs), BF16),
            V((U, Cl, Cs), BF16), V((U, Cl, Cs), BF16), V((2, U, Cl, Cs), BF16), V((U, Cl, Cs), F32), V((Cl, Cs), BF16),
            D((4,)), D(()), D((F,)), D(()), D(()), D((2, 2)), D((2,)), D((2,)), D((2,)),
            D((2,)), D(()), D((Z - 1,)), D(()), D((Z,)), D((2,)),
            D(()), D((N,)), D(()), D((N,)), D((2,)), D((2, N)), D(()), D(()), pltpu.SemaphoreType.REGULAR((2,)),
            D((LEADS,)), D((2,)), D((2, LEADS)), D((LEADS,)),
        ],
        compiler_params=pltpu.CompilerParams(
            collective_id=0, has_side_effects=True, vmem_limit_bytes=44 * 2**20
        ),
    )(*(
        pltpu.with_memory_space_constraint(value, pltpu.HBM)
        for value in (
            latents.reshape(HW, Cl), saved_input.reshape(F * Pl, Cl), out_grad.reshape(F * Pl, Cl),
            temporal_weight, spatial_weight,
        )
    ))

    def finish(ig_ref, sums_ref, ig_out, tg_out, sg_out, sem):
        half = (taps - KT) // 2
        pairs = (
            (sums_ref.at[pl.ds(KT, half)], sg_out.at[pl.ds(0, half)]),
            (sums_ref.at[pl.ds(KT + half, taps - KT - half)], sg_out.at[pl.ds(half, taps - KT - half)]),
            (sums_ref.at[pl.ds(0, KT)], tg_out),
            (ig_ref, ig_out),
        )
        copies = [pltpu.make_async_copy(src, dst, sem.at[n]) for n, (src, dst) in enumerate(pairs)]
        for copy in copies:
            copy.start()
        for copy in copies:
            copy.wait()

    ig, tg, sg = pl.pallas_call(
        finish,
        out_shape=(
            jax.ShapeDtypeStruct((HW, Cl), BF16),
            jax.ShapeDtypeStruct((KT, Cl, Cs), F32),
            jax.ShapeDtypeStruct((taps - KT, Cl, Cs), F32),
        ),
        in_specs=[vmem] * 2,
        out_specs=(hbm,) * 3,
        scratch_shapes=[D((4,))],
        compiler_params=pltpu.CompilerParams(vmem_limit_bytes=16 * 2**20),
    )(ig, sums)
    return ig.reshape(latents.shape), tg, sg


def plain(latents, saved_input, out_grad, temporal_weight, spatial_weight):
    clips_all = latents.shape[0] * lax.axis_size("clip")
    frames_all = latents.shape[1] * lax.axis_size("sp")
    scale_factor = 1.0 / math.sqrt(clips_all * frames_all * HS * WS)
    frames_count = out_grad.shape[1]
    local_in = temporal_weight.shape[1]
    saved_padded = pad_frames(saved_input)
    block_in = lax.all_gather(out_grad, "tp", axis=3, tiled=True)
    padded = pad_frames(block_in)
    hidden_acc = jnp.zeros(out_grad.shape[:3] + (local_in,), F32)
    parts = []
    for tap_index in range(3):
        shifted = padded[:, 2 - tap_index : 2 - tap_index + frames_count]
        hidden_acc = hidden_acc + jnp.einsum(
            "bfpo,io->bfpi", shifted, temporal_weight[tap_index], preferred_element_type=F32
        )
        window = saved_padded[:, tap_index : tap_index + frames_count]
        parts.append(jnp.einsum("bfpi,bfpo->io", window, block_in, preferred_element_type=F32))
    temporal_local = jnp.stack(parts)
    hidden_grad = hidden_acc.astype(BF16)
    regrouped = lax.all_to_all(hidden_grad, "sp", split_axis=1, concat_axis=2, tiled=True)
    batch = latents.shape[0] * latents.shape[1]
    image_pad = jnp.pad(latents.reshape(batch, HS, WS, local_in), ((0, 0), (1, 1), (1, 1), (0, 0)))
    block_in = lax.all_gather(regrouped, "tp", axis=3, tiled=True)
    whole = block_in.reshape(batch, HS, WS, block_in.shape[3])
    grid = jnp.pad(whole, ((0, 0), (1, 1), (1, 1), (0, 0)))
    input_acc = jnp.zeros((batch, HS, WS, local_in), F32)
    parts = []
    for row in (-1, 0, 1):
        for col in (-1, 0, 1):
            tap_index = 3 * (row + 1) + (col + 1)
            moved = grid[:, 1 - row : 1 - row + HS, 1 - col : 1 - col + WS]
            input_acc = input_acc + jnp.einsum(
                "gabo,co->gabc", moved, spatial_weight[tap_index], preferred_element_type=F32
            )
            window = image_pad[:, 1 + row : 1 + row + HS, 1 + col : 1 + col + WS]
            parts.append(jnp.einsum("gabc,gabo->co", window, whole, preferred_element_type=F32))
    spatial_local = jnp.stack(parts)
    input_grad = input_acc.reshape(latents.shape).astype(BF16)
    temporal_grad, spatial_grad = lax.psum(
        tuple(
            lax.psum_scatter(value * scale_factor, "sp", scatter_dimension=2, tiled=True)
            for value in (temporal_local, spatial_local)
        ),
        "clip",
    )
    return input_grad, temporal_grad, spatial_grad


PARTS = [4, 4, 2, 2, 2, 2, 2, 2, 2, 2, 4]
HOP = 2.1
START = -0.7
LEAD = -2.6
LEADS = 4
NEAR = 3.0
EARLY = 1.5
SLACK = 0.3
LATE = {5: 4.0, "E": 4.0}
FIRST = [4, 3, 5, 0, 1, 2, 6, 7, 8]


def solution(mesh):
    sizes = (mesh.shape["sp"], mesh.shape["tp"], mesh.shape["clip"])

    def local(latents, saved_input, out_grad, temporal_weight, spatial_weight):
        S, T, Z = sizes
        cols = temporal_weight.shape[2] // S
        fits = (
            latents.shape[:2] == (1, 1) and S == out_grad.shape[1] == 4 and T == 2 and Z == 4
            and cols % 128 == 0 and out_grad.shape[3] % 256 == 0 and out_grad.shape[2] % 128 == 0
            and latents.shape[2] == HS * WS == S * out_grad.shape[2]
        )
        args = (latents, saved_input, out_grad, temporal_weight, spatial_weight)
        return fused(sizes, *args) if fits else plain(*args)

    return jax.shard_map(
        local,
        mesh=mesh,
        in_specs=(
            P("clip", "sp", None, "tp"),
            P("clip", None, "sp", "tp"),
            P("clip", None, "sp", "tp"),
            P(None, "tp", None),
            P(None, "tp", None),
        ),
        out_specs=(P("clip", "sp", None, "tp"), P(None, "tp", "sp"), P(None, "tp", "sp")),
        check_vma=False,
    )
```
